512 devices in a mesh: seq: 64 (over z_hi, x, y), width: 8 (over z_lo, core).
Axes of the slice: x: 4, y: 8, z: 8 (z_hi: 2, z_lo: 4; z = z_hi * 4 + z_lo), core: 2. Of those that a mesh axis runs over, the one named last changes fastest.
Arguments:
- projected: bfloat16 [32768, 3, 4096], P('seq', None, 'width'), may hold values from -6 to 6
- short_filter: float32 [3, 3, 4096], P(None, None, 'width'), may hold values from -3.5 to 3.5
- long_filter: bfloat16 [256, 128], P('width'), may hold values from -0.5 to 0.5
- out_weight: bfloat16 [4096, 4096], P('seq', 'width'), may hold values from -0.09375 to 0.09375
Outputs:
- mixed: bfloat16 [32768, 4096], P('seq', 'width')
The draws below stay inside these ranges and needn't reach their ends.
All inputs are finite; a program needn't handle non-finite values.
Results may differ from the reference program's by a relative error of at most 0.0057.
Values may be sent and summed in bfloat16 or wider, within the bound.
No kernel may reach another device: no remote copies, remote signals or barrier semaphores. Data moves between devices by JAX's collectives and lax.ppermute only.
A program may use at most 64 MiB of HBM per device.

```python
import jax
import jax.numpy as jnp
from jax import lax

C = 4096
OUT = 4096
FILT = 128
TOKENS = 32768
GROUPS = 256


def steps_of(own_key, extent, cuts, low, largest):
    factor_of = 1.0
    for position, shards_of in cuts:
        heights = jax.random.uniform(jax.random.fold_in(jax.random.fold_in(own_key, 6), position), (shards_of,), jnp.float32, low / len(cuts), largest / len(cuts))
        factor_of = factor_of * jnp.repeat(jnp.exp(heights), extent[position] // shards_of).reshape((-1,) + (1,) * (len(extent) - 1 - position))
    return factor_of


def bell_draw(key, shape, width, reach, shards=(), kind=jnp.bfloat16):
    loudness = steps_of(key, shape, shards, -0.22, 0.18) if shards else 1.0
    result = jax.random.normal(key, shape, jnp.float32) * width * loudness
    return jnp.minimum(jnp.maximum(result, -reach), reach).astype(kind)


def setup_inputs(seed: int = 0) -> dict:
    streams_of = jax.random.split(jax.random.key(seed), 5)
    return {
        "projected": bell_draw(streams_of[0], (TOKENS, 3, C), 1.0, 6.0, ((0, 64), (2, 8))),
        "short_filter": bell_draw(streams_of[1], (3, 3, C), 3 ** -0.5, 3.5, ((2, 8),), jnp.float32),
        "long_filter": bell_draw(streams_of[2], (GROUPS, FILT), FILT ** -0.5, 0.5, ((0, 8),)),
        "out_weight": bell_draw(streams_of[3], (C, OUT), C ** -0.5, 0.09375, ((0, 64), (1, 8))),
    }


def featurize(projected, short_filter):
    values = projected.astype(jnp.float32)
    padded = jnp.pad(values, ((2, 0), (0, 0), (0, 0)))
    return short_filter[0] * padded[2:] + short_filter[1] * padded[1:-1] + short_filter[2] * padded[:-2]


def toeplitz_of(long_filter):
    span = long_filter.shape[1]
    row_ids = jnp.arange(span, dtype=jnp.int32)[:, None]
    col_ids = jnp.arange(2 * span - 1, dtype=jnp.int32)[None, :]
    tap_index = row_ids - col_ids + (span - 1)
    inside = (tap_index >= 0) & (tap_index < span)
    picked = jnp.take(long_filter, jnp.clip(tap_index, 0, span - 1), axis=1)
    return jnp.where(inside[None], picked, jnp.zeros_like(picked))


def long_conv(extended, toeplitz, out_rows):
    span = toeplitz.shape[1]
    groups = toeplitz.shape[0]
    channels = extended.shape[1]
    toeplitz_wide = toeplitz.astype(jnp.float32)

    def one_block(block_index):
        window_rows = lax.dynamic_slice_in_dim(extended, block_index * span, 2 * span - 1, 0)
        window_rows = window_rows.reshape(2 * span - 1, groups, channels // groups).astype(jnp.float32)
        return jnp.einsum("gij,jgc->igc", toeplitz_wide, window_rows).reshape(span, channels)

    blocks = lax.map(one_block, jnp.arange(out_rows // span, dtype=jnp.int32))
    return blocks.reshape(out_rows, channels)


def reference(projected, short_filter, long_filter, out_weight):
    featured = featurize(projected, short_filter)
    product = (featured[:, 1] * featured[:, 2]).astype(jnp.bfloat16)
    span = long_filter.shape[1]
    extended = jnp.pad(product, ((span - 1, 0), (0, 0)))
    filtered = long_conv(extended, toeplitz_of(long_filter), product.shape[0])
    gated = (featured[:, 0] * filtered).astype(jnp.bfloat16)
    return jnp.dot(gated, out_weight, preferred_element_type=jnp.float32).astype(jnp.bfloat16)
```

```python
import jax
import jax.numpy as jnp
from jax import lax
from jax.sharding import Mesh
from jax.sharding import PartitionSpec as P

SEQ_PARTS = (("zh", 2), ("x", 4), ("y", 8))
WIDTH_PARTS = (("zl", 4), ("c", 2))
SEQ = tuple(n for n, _ in SEQ_PARTS)
WIDTH = tuple(n for n, _ in WIDTH_PARTS)


def from_behind(array):
    total = 1
    for _, size in SEQ_PARTS:
        total *= size
    pairs = [(i, i + 1) for i in range(total - 1)]
    return lax.ppermute(array, SEQ, pairs)


def toeplitz_blocks(long_filter):
    groups, span = long_filter.shape
    period = 3 * span
    row = jnp.concatenate(
        [
            jnp.zeros((groups, 1), long_filter.dtype),
            long_filter[:, ::-1],
            jnp.zeros((groups, period - span - 1), long_filter.dtype),
        ],
        axis=1,
    )
    tiled = jnp.broadcast_to(row[:, None, :], (groups, span, period))
    flat = tiled.reshape(groups, span * period)[:, : span * (period - 1)]
    return flat.reshape(groups, span, period - 1)[:, :, : 2 * span]


def on_device(projected, short_filter, long_filter, out_weight):
    tok_rows = projected.shape[0]
    groups, span = long_filter.shape
    channels = projected.shape[2]

    partner = lax.ppermute(out_weight, "zh", [(0, 1), (1, 0)])
    zh = lax.axis_index("zh")
    pair = jnp.where(zh == 0, jnp.stack([out_weight, partner]), jnp.stack([partner, out_weight]))
    weight_xy = lax.all_gather(pair, ("x", "y"), axis=0, tiled=False)
    weight = jnp.transpose(weight_xy, (1, 0, 2, 3)).reshape(-1, weight_xy.shape[-1])

    tail = projected[tok_rows - span - 2 :]
    previous = from_behind(tail)
    joined = jnp.concatenate([previous, projected], axis=0).astype(jnp.float32)
    featured = (
        short_filter[0] * joined[2:]
        + short_filter[1] * joined[1:-1]
        + short_filter[2] * joined[:-2]
    )
    product = (featured[:, 1] * featured[:, 2]).astype(jnp.bfloat16)
    query = featured[span:, 0]

    blocks = product.reshape(tok_rows // span + 1, span, groups, channels // groups)
    window = jnp.concatenate([blocks[:-1], blocks[1:]], axis=1)
    toeplitz = toeplitz_blocks(long_filter)
    filtered = jnp.einsum(
        "gij,bjgc->bigc", toeplitz, window, preferred_element_type=jnp.float32
    ).reshape(tok_rows, channels)
    gated = (query * filtered).astype(jnp.bfloat16)

    g_zl = lax.all_gather(gated, "zl", axis=1, tiled=False)
    g_all = lax.all_gather(g_zl, "c", axis=2, tiled=False)
    gathered = g_all.reshape(tok_rows, -1)

    mixed = jnp.dot(gathered, weight, preferred_element_type=jnp.float32)
    return mixed.astype(jnp.bfloat16)


def solution(mesh):
    names = SEQ + WIDTH
    sizes = tuple(s for _, s in SEQ_PARTS + WIDTH_PARTS)
    fine = Mesh(mesh.devices.reshape(sizes), names)
    in_specs = (
        P(SEQ, None, WIDTH),
        P(None, None, WIDTH),
        P(WIDTH, None),
        P(SEQ, WIDTH),
    )
    out_specs = P(SEQ, WIDTH)
    return jax.shard_map(
        on_device, mesh=fine, in_specs=in_specs, out_specs=out_specs, check_vma=False
    )
```

```python
import jax
import jax.numpy as jnp
from jax import lax
from jax.experimental import pallas as pl
from jax.experimental.pallas import tpu as pltpu
from jax.sharding import Mesh
from jax.sharding import PartitionSpec as P

SEQ_PARTS = (("zh", 2), ("x", 4), ("y", 8))
WIDTH_PARTS = (("zl", 4), ("c", 2))
SEQ = tuple(n for n, _ in SEQ_PARTS)
WIDTH = tuple(n for n, _ in WIDTH_PARTS)


def from_behind(array):
    total = 1
    for _, size in SEQ_PARTS:
        total *= size
    pairs = [(i, i + 1) for i in range(total - 1)]
    return lax.ppermute(array, SEQ, pairs)


def toeplitz_kernel(row_ref, out_ref):
    groups, span, width = out_ref.shape
    period = row_ref.shape[1]

    def one_group(g, carry):
        row = row_ref[pl.ds(g, 1), :]
        tiled = jnp.broadcast_to(row, (span, period))
        rolled = pltpu.roll(tiled, shift=0, axis=1, stride=1, stride_axis=0)
        out_ref[g] = rolled[:, :width].astype(out_ref.dtype)
        return carry

    lax.fori_loop(0, groups, one_group, 0)


def toeplitz_blocks(long_filter):
    groups, span = long_filter.shape
    period = 3 * span
    row = jnp.concatenate(
        [
            jnp.zeros((groups, 1), jnp.float32),
            long_filter[:, ::-1].astype(jnp.float32),
            jnp.zeros((groups, period - span - 1), jnp.float32),
        ],
        axis=1,
    )
    return pl.pallas_call(
        toeplitz_kernel,
        out_shape=jax.ShapeDtypeStruct((groups, span, 2 * span), long_filter.dtype),
    )(row)


def line_gather(block, axis_name, size):
    pieces = [None] * size
    index = lax.axis_index(axis_name)
    received = {}
    for offset in range(1, size):
        for sign in (1, -1):
            d = sign * offset
            pairs = [(i, i + d) for i in range(size) if 0 <= i + d < size]
            received[d] = lax.ppermute(block, axis_name, pairs)
    parts = []
    for source in range(size):
        choice = jnp.zeros_like(block)
        for d, value in received.items():
            choice = jnp.where(index - d == source, value, choice)
        parts.append(jnp.where(index == source, block, choice))
    return jnp.stack(parts, axis=1)


def on_device(projected, short_filter, long_filter, out_weight):
    tok_rows = projected.shape[0]
    groups, span = long_filter.shape
    channels = projected.shape[2]

    partner = lax.ppermute(out_weight, "zh", [(0, 1), (1, 0)])
    zh = lax.axis_index("zh")
    pair = jnp.where(zh == 0, jnp.stack([out_weight, partner]), jnp.stack([partner, out_weight]))
    weight_xy = lax.all_gather(pair, ("x", "y"), axis=0, tiled=False)
    weight = jnp.transpose(weight_xy, (1, 0, 2, 3)).reshape(-1, weight_xy.shape[-1])

    tail = projected[tok_rows - span - 2 :]
    previous = from_behind(tail)
    joined = jnp.concatenate([previous, projected], axis=0).astype(jnp.float32)
    featured = (
        short_filter[0] * joined[2:]
        + short_filter[1] * joined[1:-1]
        + short_filter[2] * joined[:-2]
    )
    product = (featured[:, 1] * featured[:, 2]).astype(jnp.bfloat16)
    query = featured[span:, 0]

    blocks = product.reshape(tok_rows // span + 1, span, groups, channels // groups)
    window = jnp.concatenate([blocks[:-1], blocks[1:]], axis=1)
    toeplitz = toeplitz_blocks(long_filter)
    filtered = jnp.einsum(
        "gij,bjgc->bigc", toeplitz, window, preferred_element_type=jnp.float32
    ).reshape(tok_rows, channels)
    gated = (query * filtered).astype(jnp.bfloat16)

    g_zl = line_gather(gated, "zl", 4)
    other = lax.ppermute(g_zl, "c", [(0, 1), (1, 0)])
    core = lax.axis_index("c")
    g_all = jnp.where(core == 0, jnp.stack([g_zl, other], axis=2), jnp.stack([other, g_zl], axis=2))
    gathered = g_all.reshape(tok_rows, -1)

    mixed = jnp.dot(gathered, weight, preferred_element_type=jnp.float32)
    return mixed.astype(jnp.bfloat16)


def solution(mesh):
    names = SEQ + WIDTH
    sizes = tuple(s for _, s in SEQ_PARTS + WIDTH_PARTS)
    fine = Mesh(mesh.devices.reshape(sizes), names)
    in_specs = (
        P(SEQ, None, WIDTH),
        P(None, None, WIDTH),
        P(WIDTH, None),
        P(SEQ, WIDTH),
    )
    out_specs = P(SEQ, WIDTH)
    return jax.shard_map(
        on_device, mesh=fine, in_specs=in_specs, out_specs=out_specs, check_vma=False
    )
```

```python
import jax
import jax.numpy as jnp
from jax import lax
from jax.experimental import pallas as pl
from jax.experimental.pallas import tpu as pltpu
from jax.sharding import Mesh
from jax.sharding import PartitionSpec as P

SEQ_PARTS = (("zh", 2), ("x", 4), ("y", 8))
WIDTH_PARTS = (("zl", 4), ("c", 2))
SEQ = tuple(n for n, _ in SEQ_PARTS)
WIDTH = tuple(n for n, _ in WIDTH_PARTS)


def from_behind(array):
    total = 1
    for _, size in SEQ_PARTS:
        total *= size
    pairs = [(i, i + 1) for i in range(total - 1)]
    return lax.ppermute(array, SEQ, pairs)


def toeplitz_kernel(row_ref, out_ref):
    groups, span, width = out_ref.shape
    period = row_ref.shape[1]

    def one_group(g, carry):
        row = row_ref[pl.ds(g, 1), :]
        tiled = jnp.broadcast_to(row, (span, period))
        rolled = pltpu.roll(tiled, shift=0, axis=1, stride=1, stride_axis=0)
        out_ref[g] = rolled[:, :width].astype(out_ref.dtype)
        return carry

    lax.fori_loop(0, groups, one_group, 0)


def toeplitz_blocks(long_filter):
    groups, span = long_filter.shape
    period = 3 * span
    row = jnp.concatenate(
        [
            jnp.zeros((groups, 1), jnp.float32),
            long_filter[:, ::-1].astype(jnp.float32),
            jnp.zeros((groups, period - span - 1), jnp.float32),
        ],
        axis=1,
    )
    return pl.pallas_call(
        toeplitz_kernel,
        out_shape=jax.ShapeDtypeStruct((groups, span, 2 * span), long_filter.dtype),
    )(row)


def line_gather(block, axis_name, size):
    pieces = [None] * size
    index = lax.axis_index(axis_name)
    received = {}
    for offset in range(1, size):
        for sign in (1, -1):
            d = sign * offset
            pairs = [(i, i + d) for i in range(size) if 0 <= i + d < size]
            received[d] = lax.ppermute(block, axis_name, pairs)
    parts = []
    for source in range(size):
        choice = jnp.zeros_like(block)
        for d, value in received.items():
            choice = jnp.where(index - d == source, value, choice)
        parts.append(jnp.where(index == source, block, choice))
    return jnp.stack(parts, axis=1)


def on_device(projected, short_filter, long_filter, out_weight):
    tok_rows = projected.shape[0]
    groups, span = long_filter.shape
    channels = projected.shape[2]

    partner = lax.ppermute(out_weight, "zh", [(0, 1), (1, 0)])
    tail = projected[tok_rows - span - 2 :]
    previous = from_behind(tail)
    partner, previous = lax.optimization_barrier((partner, previous))

    zh = lax.axis_index("zh")
    pair = jnp.where(zh == 0, jnp.stack([out_weight, partner]), jnp.stack([partner, out_weight]))
    weight_y = lax.all_gather(pair, "y", axis=0, tiled=False)

    joined = jnp.concatenate([previous, projected], axis=0).astype(jnp.float32)
    featured = (
        short_filter[0] * joined[2:]
        + short_filter[1] * joined[1:-1]
        + short_filter[2] * joined[:-2]
    )
    product = (featured[:, 1] * featured[:, 2]).astype(jnp.bfloat16)
    query = featured[span:, 0]

    blocks = product.reshape(tok_rows // span + 1, span, groups, channels // groups)
    window = jnp.concatenate([blocks[:-1], blocks[1:]], axis=1)
    toeplitz = toeplitz_blocks(long_filter)
    filtered = jnp.einsum(
        "gij,bjgc->bigc", toeplitz, window, preferred_element_type=jnp.float32
    ).reshape(tok_rows, channels)
    gated = (query * filtered).astype(jnp.bfloat16)

    weight_y, gated = lax.optimization_barrier((weight_y, gated))
    weight_xy = lax.all_gather(weight_y, "x", axis=0, tiled=False)

    g_zl = line_gather(gated, "zl", 4)
    other = lax.ppermute(g_zl, "c", [(0, 1), (1, 0)])
    core = lax.axis_index("c")
    out_cols = weight_xy.shape[-1]

    def weight_rows(zl, c):
        x = 2 * (zl % 2) + c
        piece = lax.dynamic_index_in_dim(weight_xy, x, axis=0, keepdims=False)[:, zl // 2]
        return piece.reshape(-1, out_cols)

    mixed = jnp.zeros((tok_rows, out_cols), jnp.float32)
    for zl in range(4):
        mixed = mixed + jnp.dot(g_zl[:, zl], weight_rows(zl, core), preferred_element_type=jnp.float32)
    for zl in range(4):
        mixed = mixed + jnp.dot(other[:, zl], weight_rows(zl, 1 - core), preferred_element_type=jnp.float32)
    return mixed.astype(jnp.bfloat16)


def solution(mesh):
    names = SEQ + WIDTH
    sizes = tuple(s for _, s in SEQ_PARTS + WIDTH_PARTS)
    fine = Mesh(mesh.devices.reshape(sizes), names)
    in_specs = (
        P(SEQ, None, WIDTH),
        P(None, None, WIDTH),
        P(WIDTH, None),
        P(SEQ, WIDTH),
    )
    out_specs = P(SEQ, WIDTH)
    return jax.shard_map(
        on_device, mesh=fine, in_specs=in_specs, out_specs=out_specs, check_vma=False
    )
```

```python
import jax
import jax.numpy as jnp
from jax import lax
from jax.experimental import pallas as pl
from jax.experimental.pallas import tpu as pltpu
from jax.sharding import Mesh
from jax.sharding import PartitionSpec as P

SEQ_PARTS = (("zh", 2), ("x", 4), ("y", 8))
WIDTH_PARTS = (("zl", 4), ("c", 2))
SEQ = tuple(n for n, _ in SEQ_PARTS)
WIDTH = tuple(n for n, _ in WIDTH_PARTS)


def from_behind(array):
    total = 1
    for _, size in SEQ_PARTS:
        total *= size
    pairs = [(i, i + 1) for i in range(total - 1)]
    return lax.ppermute(array, SEQ, pairs)


def toeplitz_kernel(row_ref, out_ref):
    groups, span, width = out_ref.shape
    period = row_ref.shape[1]

    def one_group(g, carry):
        row = row_ref[pl.ds(g, 1), :]
        tiled = jnp.broadcast_to(row, (span, period))
        rolled = pltpu.roll(tiled, shift=0, axis=1, stride=1, stride_axis=0)
        out_ref[g] = rolled[:, :width].astype(out_ref.dtype)
        return carry

    lax.fori_loop(0, groups, one_group, 0)


def toeplitz_blocks(long_filter):
    groups, span = long_filter.shape
    period = 3 * span
    row = jnp.concatenate(
        [
            jnp.zeros((groups, 1), jnp.float32),
            long_filter[:, ::-1].astype(jnp.float32),
            jnp.zeros((groups, period - span - 1), jnp.float32),
        ],
        axis=1,
    )
    return pl.pallas_call(
        toeplitz_kernel,
        out_shape=jax.ShapeDtypeStruct((groups, span, 2 * span), long_filter.dtype),
    )(row)


def line_gather(block, axis_name, size):
    pieces = [None] * size
    index = lax.axis_index(axis_name)
    received = {}
    for offset in range(1, size):
        for sign in (1, -1):
            d = sign * offset
            pairs = [(i, i + d) for i in range(size) if 0 <= i + d < size]
            received[d] = lax.ppermute(block, axis_name, pairs)
    parts = []
    for source in range(size):
        choice = jnp.zeros_like(block)
        for d, value in received.items():
            choice = jnp.where(index - d == source, value, choice)
        parts.append(jnp.where(index == source, block, choice))
    return jnp.stack(parts, axis=1)


def on_device(projected, short_filter, long_filter, out_weight):
    tok_rows = projected.shape[0]
    groups, span = long_filter.shape
    channels = projected.shape[2]

    partner = lax.ppermute(out_weight, "zh", [(0, 1), (1, 0)])
    tail = projected[tok_rows - span - 2 :]
    previous = from_behind(tail)
    partner, previous = lax.optimization_barrier((partner, previous))

    zh = lax.axis_index("zh")
    pair = jnp.where(zh == 0, jnp.stack([out_weight, partner]), jnp.stack([partner, out_weight]))
    weight_xy = lax.all_gather(pair, ("x", "y"), axis=0, tiled=False)
    weight_xy = weight_xy.reshape(4, 8, *weight_xy.shape[1:])

    joined = jnp.concatenate([previous, projected], axis=0).astype(jnp.float32)
    featured = (
        short_filter[0] * joined[2:]
        + short_filter[1] * joined[1:-1]
        + short_filter[2] * joined[:-2]
    )
    product = (featured[:, 1] * featured[:, 2]).astype(jnp.bfloat16)
    query = featured[span:, 0]

    blocks = product.reshape(tok_rows // span + 1, span, groups, channels // groups)
    window = jnp.concatenate([blocks[:-1], blocks[1:]], axis=1)
    toeplitz = toeplitz_blocks(long_filter)
    filtered = jnp.einsum(
        "gij,bjgc->bigc", toeplitz, window, preferred_element_type=jnp.float32
    ).reshape(tok_rows, channels)
    gated = (query * filtered).astype(jnp.bfloat16)

    g_zl = line_gather(gated, "zl", 4)
    other = lax.ppermute(g_zl, "c", [(0, 1), (1, 0)])
    core = lax.axis_index("c")
    out_cols = weight_xy.shape[-1]

    def weight_rows(zl, c):
        x = 2 * (zl % 2) + c
        piece = lax.dynamic_index_in_dim(weight_xy, x, axis=0, keepdims=False)[:, zl // 2]
        return piece.reshape(-1, out_cols)

    mixed = jnp.zeros((tok_rows, out_cols), jnp.float32)
    for zl in range(4):
        mixed = mixed + jnp.dot(g_zl[:, zl], weight_rows(zl, core), preferred_element_type=jnp.float32)
    for zl in range(4):
        mixed = mixed + jnp.dot(other[:, zl], weight_rows(zl, 1 - core), preferred_element_type=jnp.float32)
    return mixed.astype(jnp.bfloat16)


def solution(mesh):
    names = SEQ + WIDTH
    sizes = tuple(s for _, s in SEQ_PARTS + WIDTH_PARTS)
    fine = Mesh(mesh.devices.reshape(sizes), names)
    in_specs = (
        P(SEQ, None, WIDTH),
        P(None, None, WIDTH),
        P(WIDTH, None),
        P(SEQ, WIDTH),
    )
    out_specs = P(SEQ, WIDTH)
    return jax.shard_map(
        on_device, mesh=fine, in_specs=in_specs, out_specs=out_specs, check_vma=False
    )
```

```python
import jax
import jax.numpy as jnp
from jax import lax
from jax.experimental import pallas as pl
from jax.experimental.pallas import tpu as pltpu
from jax.sharding import Mesh
from jax.sharding import PartitionSpec as P

SEQ_PARTS = (("zh", 2), ("x", 4), ("y", 8))
WIDTH_PARTS = (("zl", 4), ("c", 2))
SEQ = tuple(n for n, _ in SEQ_PARTS)
WIDTH = tuple(n for n, _ in WIDTH_PARTS)


def from_behind(array):
    total = 1
    for _, size in SEQ_PARTS:
        total *= size
    pairs = [(i, i + 1) for i in range(total - 1)]
    return lax.ppermute(array, SEQ, pairs)


def toeplitz_kernel(row_ref, out_ref):
    groups, span, width = out_ref.shape
    period = row_ref.shape[1]

    def one_group(g, carry):
        row = row_ref[pl.ds(g, 1), :]
        tiled = jnp.broadcast_to(row, (span, period))
        rolled = pltpu.roll(tiled, shift=0, axis=1, stride=1, stride_axis=0)
        out_ref[g] = rolled[:, :width].astype(out_ref.dtype)
        return carry

    lax.fori_loop(0, groups, one_group, 0)


def toeplitz_blocks(long_filter):
    groups, span = long_filter.shape
    period = 3 * span
    row = jnp.concatenate(
        [
            jnp.zeros((groups, 1), jnp.float32),
            long_filter[:, ::-1].astype(jnp.float32),
            jnp.zeros((groups, period - span - 1), jnp.float32),
        ],
        axis=1,
    )
    return pl.pallas_call(
        toeplitz_kernel,
        out_shape=jax.ShapeDtypeStruct((groups, span, 2 * span), long_filter.dtype),
    )(row)


def line_gather(block, axis_name, size):
    pieces = [None] * size
    index = lax.axis_index(axis_name)
    received = {}
    for offset in range(1, size):
        for sign in (1, -1):
            d = sign * offset
            pairs = [(i, i + d) for i in range(size) if 0 <= i + d < size]
            received[d] = lax.ppermute(block, axis_name, pairs)
    parts = []
    for source in range(size):
        choice = jnp.zeros_like(block)
        for d, value in received.items():
            choice = jnp.where(index - d == source, value, choice)
        parts.append(jnp.where(index == source, block, choice))
    return jnp.stack(parts, axis=1)


def on_device(projected, short_filter, long_filter, out_weight):
    tok_rows = projected.shape[0]
    groups, span = long_filter.shape
    channels = projected.shape[2]

    partner = lax.ppermute(out_weight, "zh", [(0, 1), (1, 0)])
    tail = projected[tok_rows - span - 2 :]
    previous = from_behind(tail)
    partner, previous = lax.optimization_barrier((partner, previous))

    zh = lax.axis_index("zh")
    pair = jnp.where(zh == 0, jnp.stack([out_weight, partner]), jnp.stack([partner, out_weight]))
    spread = jnp.broadcast_to(pair[None], (32, *pair.shape))
    weight_xy = lax.all_to_all(spread, ("x", "y"), 0, 0, tiled=True)
    weight_xy = weight_xy.reshape(4, 8, *weight_xy.shape[1:])

    joined = jnp.concatenate([previous, projected], axis=0).astype(jnp.float32)
    featured = (
        short_filter[0] * joined[2:]
        + short_filter[1] * joined[1:-1]
        + short_filter[2] * joined[:-2]
    )
    product = (featured[:, 1] * featured[:, 2]).astype(jnp.bfloat16)
    query = featured[span:, 0]

    blocks = product.reshape(tok_rows // span + 1, span, groups, channels // groups)
    window = jnp.concatenate([blocks[:-1], blocks[1:]], axis=1)
    toeplitz = toeplitz_blocks(long_filter)
    filtered = jnp.einsum(
        "gij,bjgc->bigc", toeplitz, window, preferred_element_type=jnp.float32
    ).reshape(tok_rows, channels)
    gated = (query * filtered).astype(jnp.bfloat16)

    g_zl = line_gather(gated, "zl", 4)
    other = lax.ppermute(g_zl, "c", [(0, 1), (1, 0)])
    core = lax.axis_index("c")
    out_cols = weight_xy.shape[-1]

    def weight_rows(zl, c):
        x = 2 * (zl % 2) + c
        piece = lax.dynamic_index_in_dim(weight_xy, x, axis=0, keepdims=False)[:, zl // 2]
        return piece.reshape(-1, out_cols)

    mixed = jnp.zeros((tok_rows, out_cols), jnp.float32)
    for zl in range(4):
        mixed = mixed + jnp.dot(g_zl[:, zl], weight_rows(zl, core), preferred_element_type=jnp.float32)
    for zl in range(4):
        mixed = mixed + jnp.dot(other[:, zl], weight_rows(zl, 1 - core), preferred_element_type=jnp.float32)
    return mixed.astype(jnp.bfloat16)


def solution(mesh):
    names = SEQ + WIDTH
    sizes = tuple(s for _, s in SEQ_PARTS + WIDTH_PARTS)
    fine = Mesh(mesh.devices.reshape(sizes), names)
    in_specs = (
        P(SEQ, None, WIDTH),
        P(None, None, WIDTH),
        P(WIDTH, None),
        P(SEQ, WIDTH),
    )
    out_specs = P(SEQ, WIDTH)
    return jax.shard_map(
        on_device, mesh=fine, in_specs=in_specs, out_specs=out_specs, check_vma=False
    )
```

```python
import jax
import jax.numpy as jnp
from jax import lax
from jax.experimental import pallas as pl
from jax.experimental.pallas import tpu as pltpu
from jax.sharding import Mesh
from jax.sharding import PartitionSpec as P

SEQ_PARTS = (("zh", 2), ("x", 4), ("y", 8))
WIDTH_PARTS = (("zl", 4), ("c", 2))
SEQ = tuple(n for n, _ in SEQ_PARTS)
WIDTH = tuple(n for n, _ in WIDTH_PARTS)


def from_behind(array):
    total = 1
    for _, size in SEQ_PARTS:
        total *= size
    pairs = [(i, i + 1) for i in range(total - 1)]
    return lax.ppermute(array, SEQ, pairs)


def toeplitz_kernel(row_ref, out_ref):
    groups, span, width = out_ref.shape
    period = row_ref.shape[1]

    def one_group(g, carry):
        row = row_ref[pl.ds(g, 1), :]
        tiled = jnp.broadcast_to(row, (span, period))
        rolled = pltpu.roll(tiled, shift=0, axis=1, stride=1, stride_axis=0)
        out_ref[g] = rolled[:, :width].astype(out_ref.dtype)
        return carry

    lax.fori_loop(0, groups, one_group, 0)


def toeplitz_blocks(long_filter):
    groups, span = long_filter.shape
    period = 3 * span
    row = jnp.concatenate(
        [
            jnp.zeros((groups, 1), jnp.float32),
            long_filter[:, ::-1].astype(jnp.float32),
            jnp.zeros((groups, period - span - 1), jnp.float32),
        ],
        axis=1,
    )
    return pl.pallas_call(
        toeplitz_kernel,
        out_shape=jax.ShapeDtypeStruct((groups, span, 2 * span), long_filter.dtype),
    )(row)


def line_gather(block, axis_name, size):
    pieces = [None] * size
    index = lax.axis_index(axis_name)
    received = {}
    for offset in range(1, size):
        for sign in (1, -1):
            d = sign * offset
            pairs = [(i, i + d) for i in range(size) if 0 <= i + d < size]
            received[d] = lax.ppermute(block, axis_name, pairs)
    parts = []
    for source in range(size):
        choice = jnp.zeros_like(block)
        for d, value in received.items():
            choice = jnp.where(index - d == source, value, choice)
        parts.append(jnp.where(index == source, block, choice))
    return jnp.stack(parts, axis=1)


def on_device(projected, short_filter, long_filter, out_weight):
    tok_rows = projected.shape[0]
    groups, span = long_filter.shape
    channels = projected.shape[2]

    partner = lax.ppermute(out_weight, "zh", [(0, 1), (1, 0)])
    tail = projected[tok_rows - span - 2 :]
    previous = from_behind(tail)
    partner, previous = lax.optimization_barrier((partner, previous))

    own_xy = lax.all_gather(out_weight, ("x", "y"), axis=0, tiled=False)
    other_xy = lax.all_gather(partner, ("x", "y"), axis=0, tiled=False)
    zh = lax.axis_index("zh")
    own_xy = own_xy.reshape(4, 8, *out_weight.shape)
    other_xy = other_xy.reshape(4, 8, *out_weight.shape)

    joined = jnp.concatenate([previous, projected], axis=0).astype(jnp.float32)
    featured = (
        short_filter[0] * joined[2:]
        + short_filter[1] * joined[1:-1]
        + short_filter[2] * joined[:-2]
    )
    product = (featured[:, 1] * featured[:, 2]).astype(jnp.bfloat16)
    query = featured[span:, 0]

    blocks = product.reshape(tok_rows // span + 1, span, groups, channels // groups)
    window = jnp.concatenate([blocks[:-1], blocks[1:]], axis=1)
    toeplitz = toeplitz_blocks(long_filter)
    filtered = jnp.einsum(
        "gij,bjgc->bigc", toeplitz, window, preferred_element_type=jnp.float32
    ).reshape(tok_rows, channels)
    gated = (query * filtered).astype(jnp.bfloat16)

    g_zl = line_gather(gated, "zl", 4)
    other = lax.ppermute(g_zl, "c", [(0, 1), (1, 0)])
    core = lax.axis_index("c")
    out_cols = out_weight.shape[-1]

    def weight_rows(zl, c):
        x = 2 * (zl % 2) + c
        own = lax.dynamic_index_in_dim(own_xy, x, axis=0, keepdims=False)
        other = lax.dynamic_index_in_dim(other_xy, x, axis=0, keepdims=False)
        piece = jnp.where(zh == zl // 2, own, other)
        return piece.reshape(-1, out_cols)

    mixed = jnp.zeros((tok_rows, out_cols), jnp.float32)
    for zl in range(4):
        mixed = mixed + jnp.dot(g_zl[:, zl], weight_rows(zl, core), preferred_element_type=jnp.float32)
    for zl in range(4):
        mixed = mixed + jnp.dot(other[:, zl], weight_rows(zl, 1 - core), preferred_element_type=jnp.float32)
    return mixed.astype(jnp.bfloat16)


def solution(mesh):
    names = SEQ + WIDTH
    sizes = tuple(s for _, s in SEQ_PARTS + WIDTH_PARTS)
    fine = Mesh(mesh.devices.reshape(sizes), names)
    in_specs = (
        P(SEQ, None, WIDTH),
        P(None, None, WIDTH),
        P(WIDTH, None),
        P(SEQ, WIDTH),
    )
    out_specs = P(SEQ, WIDTH)
    return jax.shard_map(
        on_device, mesh=fine, in_specs=in_specs, out_specs=out_specs, check_vma=False
    )
```

```python
import jax
import jax.numpy as jnp
from jax import lax
from jax.experimental import pallas as pl
from jax.experimental.pallas import tpu as pltpu
from jax.sharding import Mesh
from jax.sharding import PartitionSpec as P

SEQ_PARTS = (("zh", 2), ("x", 4), ("y", 8))
WIDTH_PARTS = (("zl", 4), ("c", 2))
SEQ = tuple(n for n, _ in SEQ_PARTS)
WIDTH = tuple(n for n, _ in WIDTH_PARTS)


def from_behind(array):
    total = 1
    for _, size in SEQ_PARTS:
        total *= size
    pairs = [(i, i + 1) for i in range(total - 1)]
    return lax.ppermute(array, SEQ, pairs)


def toeplitz_kernel(row_ref, out_ref):
    groups, span, width = out_ref.shape
    period = row_ref.shape[1]

    def one_group(g, carry):
        row = row_ref[pl.ds(g, 1), :]
        tiled = jnp.broadcast_to(row, (span, period))
        rolled = pltpu.roll(tiled, shift=0, axis=1, stride=1, stride_axis=0)
        out_ref[g] = rolled[:, :width].astype(out_ref.dtype)
        return carry

    lax.fori_loop(0, groups, one_group, 0)


def toeplitz_blocks(long_filter):
    groups, span = long_filter.shape
    period = 3 * span
    row = jnp.concatenate(
        [
            jnp.zeros((groups, 1), jnp.float32),
            long_filter[:, ::-1].astype(jnp.float32),
            jnp.zeros((groups, period - span - 1), jnp.float32),
        ],
        axis=1,
    )
    return pl.pallas_call(
        toeplitz_kernel,
        out_shape=jax.ShapeDtypeStruct((groups, span, 2 * span), long_filter.dtype),
    )(row)


def line_gather(block, axis_name, size):
    pieces = [None] * size
    index = lax.axis_index(axis_name)
    received = {}
    for offset in range(1, size):
        for sign in (1, -1):
            d = sign * offset
            pairs = [(i, i + d) for i in range(size) if 0 <= i + d < size]
            received[d] = lax.ppermute(block, axis_name, pairs)
    parts = []
    for source in range(size):
        choice = jnp.zeros_like(block)
        for d, value in received.items():
            choice = jnp.where(index - d == source, value, choice)
        parts.append(jnp.where(index == source, block, choice))
    return jnp.stack(parts, axis=1)


def on_device(projected, short_filter, long_filter, out_weight):
    tok_rows = projected.shape[0]
    groups, span = long_filter.shape
    channels = projected.shape[2]

    partner = lax.ppermute(out_weight, "zh", [(0, 1), (1, 0)])
    zh = lax.axis_index("zh")
    pair = jnp.where(zh == 0, jnp.stack([out_weight, partner]), jnp.stack([partner, out_weight]))
    weight_xy = lax.all_gather(pair, ("x", "y"), axis=0, tiled=False)
    weight = jnp.transpose(weight_xy, (1, 0, 2, 3)).reshape(-1, weight_xy.shape[-1])

    kv_tail = projected[tok_rows - span - 2 :, 1:]
    q_tail = projected[tok_rows - 2 :, 0][None]
    received = from_behind(jnp.concatenate([kv_tail, q_tail], axis=0))
    kv = jnp.concatenate([received[: span + 2], projected[:, 1:]], axis=0).astype(jnp.float32)
    f_kv = short_filter[0, 1:] * kv[2:] + short_filter[1, 1:] * kv[1:-1] + short_filter[2, 1:] * kv[:-2]
    product = (f_kv[:, 0] * f_kv[:, 1]).astype(jnp.bfloat16)
    q = jnp.concatenate([received[span + 2], projected[:, 0]], axis=0).astype(jnp.float32)
    query = short_filter[0, 0] * q[2:] + short_filter[1, 0] * q[1:-1] + short_filter[2, 0] * q[:-2]

    blocks = product.reshape(tok_rows // span + 1, span, groups, channels // groups)
    window = jnp.concatenate([blocks[:-1], blocks[1:]], axis=1)
    toeplitz = toeplitz_blocks(long_filter)
    filtered = jnp.einsum(
        "gij,bjgc->bigc", toeplitz, window, preferred_element_type=jnp.float32
    ).reshape(tok_rows, channels)
    gated = (query * filtered).astype(jnp.bfloat16)

    g_zl = line_gather(gated, "zl", 4)
    other = lax.ppermute(g_zl, "c", [(0, 1), (1, 0)])
    core = lax.axis_index("c")
    g_all = jnp.where(core == 0, jnp.stack([g_zl, other], axis=2), jnp.stack([other, g_zl], axis=2))
    gathered = g_all.reshape(tok_rows, -1)

    mixed = jnp.dot(gathered, weight, preferred_element_type=jnp.float32)
    return mixed.astype(jnp.bfloat16)


def solution(mesh):
    names = SEQ + WIDTH
    sizes = tuple(s for _, s in SEQ_PARTS + WIDTH_PARTS)
    fine = Mesh(mesh.devices.reshape(sizes), names)
    in_specs = (
        P(SEQ, None, WIDTH),
        P(None, None, WIDTH),
        P(WIDTH, None),
        P(SEQ, WIDTH),
    )
    out_specs = P(SEQ, WIDTH)
    return jax.shard_map(
        on_device, mesh=fine, in_specs=in_specs, out_specs=out_specs, check_vma=False
    )
```

```python
import jax
import jax.numpy as jnp
from jax import lax
from jax.experimental import pallas as pl
from jax.experimental.pallas import tpu as pltpu
from jax.sharding import Mesh
from jax.sharding import PartitionSpec as P

SEQ_PARTS = (("zh", 2), ("x", 4), ("y", 8))
WIDTH_PARTS = (("zl", 4), ("c", 2))
SEQ = tuple(n for n, _ in SEQ_PARTS)
WIDTH = tuple(n for n, _ in WIDTH_PARTS)


def from_behind(array):
    total = 1
    for _, size in SEQ_PARTS:
        total *= size
    pairs = [(i, i + 1) for i in range(total - 1)]
    return lax.ppermute(array, SEQ, pairs)


def toeplitz_kernel(row_ref, out_ref):
    groups, span, width = out_ref.shape
    period = row_ref.shape[1]

    def one_group(g, carry):
        row = row_ref[pl.ds(g, 1), :]
        tiled = jnp.broadcast_to(row, (span, period))
        rolled = pltpu.roll(tiled, shift=0, axis=1, stride=1, stride_axis=0)
        out_ref[g] = rolled[:, :width].astype(out_ref.dtype)
        return carry

    lax.fori_loop(0, groups, one_group, 0)


def toeplitz_blocks(long_filter):
    groups, span = long_filter.shape
    period = 3 * span
    row = jnp.concatenate(
        [
            jnp.zeros((groups, 1), jnp.float32),
            long_filter[:, ::-1].astype(jnp.float32),
            jnp.zeros((groups, period - span - 1), jnp.float32),
        ],
        axis=1,
    )
    return pl.pallas_call(
        toeplitz_kernel,
        out_shape=jax.ShapeDtypeStruct((groups, span, 2 * span), long_filter.dtype),
    )(row)


def line_slots(block, axis_name, size):
    index = lax.axis_index(axis_name)
    received = {}
    for offset in range(1, size):
        for d in (offset, -offset):
            pairs = [(i, i + d) for i in range(size) if 0 <= i + d < size]
            received[d] = lax.ppermute(block, axis_name, pairs)
    slots = [block]
    for k in range(1, size):
        slots.append(jnp.where(index + k < size, received[-k], received[size - k]))
    return jnp.stack(slots)


def partial_kernel(table_ref, piece_ref, weight_ref, out_ref, acc_ref):
    k = pl.program_id(0)

    @pl.when(k == 0)
    def _():
        acc_ref[...] = jnp.zeros_like(acc_ref)

    rows = weight_ref[0, :, 0]
    rows = rows.reshape(-1, rows.shape[-1])
    acc_ref[...] += jnp.dot(piece_ref[0], rows, preferred_element_type=jnp.float32)

    @pl.when(k == pl.num_programs(0) - 1)
    def _():
        out_ref[...] = acc_ref[...]


def final_kernel(table_ref, piece_ref, weight_ref, carry_ref, out_ref, acc_ref):
    k = pl.program_id(0)

    @pl.when(k == 0)
    def _():
        acc_ref[...] = carry_ref[...]

    rows = weight_ref[0, :, 0]
    rows = rows.reshape(-1, rows.shape[-1])
    acc_ref[...] += jnp.dot(piece_ref[0], rows, preferred_element_type=jnp.float32)

    @pl.when(k == pl.num_programs(0) - 1)
    def _():
        out_ref[...] = acc_ref[...].astype(out_ref.dtype)


def block_matmul(table, pieces, weight, carry=None):
    n, tok, width = pieces.shape
    _, ys, _, rows, cols = weight.shape
    in_specs = [
        pl.BlockSpec((1, tok, width), lambda k, t: (k, 0, 0)),
        pl.BlockSpec((1, ys, 1, rows, cols), lambda k, t: (t[0, k], 0, t[1, k], 0, 0)),
    ]
    args = [table, pieces, weight]
    if carry is None:
        kernel, out_dtype = partial_kernel, jnp.float32
    else:
        kernel, out_dtype = final_kernel, jnp.bfloat16
        in_specs.append(pl.BlockSpec((tok, cols), lambda k, t: (0, 0)))
        args.append(carry)
    grid_spec = pltpu.PrefetchScalarGridSpec(
        num_scalar_prefetch=1,
        grid=(n,),
        in_specs=in_specs,
        out_specs=pl.BlockSpec((tok, cols), lambda k, t: (0, 0)),
        scratch_shapes=[pltpu.VMEM((tok, cols), jnp.float32)],
    )
    return pl.pallas_call(
        kernel,
        grid_spec=grid_spec,
        out_shape=jax.ShapeDtypeStruct((tok, cols), out_dtype),
    )(*args)


def on_device(projected, short_filter, long_filter, out_weight):
    tok_rows = projected.shape[0]
    groups, span = long_filter.shape
    channels = projected.shape[2]

    partner = lax.ppermute(out_weight, "zh", [(0, 1), (1, 0)])
    zh = lax.axis_index("zh")
    pair = jnp.where(zh == 0, jnp.stack([out_weight, partner]), jnp.stack([partner, out_weight]))
    weight_xy = lax.all_gather(pair, ("x", "y"), axis=0, tiled=False)

    kv_tail = projected[tok_rows - span - 2 :, 1:]
    q_tail = projected[tok_rows - 2 :, 0][None]
    received = from_behind(jnp.concatenate([kv_tail, q_tail], axis=0))
    kv = jnp.concatenate([received[: span + 2], projected[:, 1:]], axis=0).astype(jnp.float32)
    f_kv = short_filter[0, 1:] * kv[2:] + short_filter[1, 1:] * kv[1:-1] + short_filter[2, 1:] * kv[:-2]
    product = (f_kv[:, 0] * f_kv[:, 1]).astype(jnp.bfloat16)
    q = jnp.concatenate([received[span + 2], projected[:, 0]], axis=0).astype(jnp.float32)
    query = short_filter[0, 0] * q[2:] + short_filter[1, 0] * q[1:-1] + short_filter[2, 0] * q[:-2]

    blocks = product.reshape(tok_rows // span + 1, span, groups, channels // groups)
    window = jnp.concatenate([blocks[:-1], blocks[1:]], axis=1)
    toeplitz = toeplitz_blocks(long_filter)
    filtered = jnp.einsum(
        "gij,bjgc->bigc", toeplitz, window, preferred_element_type=jnp.float32
    ).reshape(tok_rows, channels)
    gated = (query * filtered).astype(jnp.bfloat16)

    own = line_slots(gated, "zl", 4)
    other = lax.ppermute(own, "c", [(0, 1), (1, 0)])
    zl = lax.axis_index("zl")
    core = lax.axis_index("c")
    sources = (zl + jnp.arange(4, dtype=jnp.int32)) % 4

    def table_for(c):
        w = 2 * sources + c
        return jnp.stack([w % 4, w // 4]).astype(jnp.int32)

    weight = weight_xy.reshape(4, 8, *weight_xy.shape[1:])
    carry = block_matmul(table_for(core), own, weight)
    return block_matmul(table_for(1 - core), other, weight, carry)


def solution(mesh):
    names = SEQ + WIDTH
    sizes = tuple(s for _, s in SEQ_PARTS + WIDTH_PARTS)
    fine = Mesh(mesh.devices.reshape(sizes), names)
    in_specs = (
        P(SEQ, None, WIDTH),
        P(None, None, WIDTH),
        P(WIDTH, None),
        P(SEQ, WIDTH),
    )
    out_specs = P(SEQ, WIDTH)
    return jax.shard_map(
        on_device, mesh=fine, in_specs=in_specs, out_specs=out_specs, check_vma=False
    )
```

```python
import jax
import jax.numpy as jnp
from jax import lax
from jax.experimental import pallas as pl
from jax.experimental.pallas import tpu as pltpu
from jax.sharding import Mesh
from jax.sharding import PartitionSpec as P

SEQ_PARTS = (("zh", 2), ("x", 4), ("y", 8))
WIDTH_PARTS = (("zl", 4), ("c", 2))
SEQ = tuple(n for n, _ in SEQ_PARTS)
WIDTH = tuple(n for n, _ in WIDTH_PARTS)


def from_behind(array):
    total = 1
    for _, size in SEQ_PARTS:
        total *= size
    pairs = [(i, i + 1) for i in range(total - 1)]
    return lax.ppermute(array, SEQ, pairs)


def toeplitz_kernel(row_ref, out_ref):
    groups, span, width = out_ref.shape
    period = row_ref.shape[1]

    def one_group(g, carry):
        row = row_ref[pl.ds(g, 1), :]
        tiled = jnp.broadcast_to(row, (span, period))
        rolled = pltpu.roll(tiled, shift=0, axis=1, stride=1, stride_axis=0)
        out_ref[g] = rolled[:, :width].astype(out_ref.dtype)
        return carry

    lax.fori_loop(0, groups, one_group, 0)


def toeplitz_blocks(long_filter):
    groups, span = long_filter.shape
    period = 3 * span
    row = jnp.concatenate(
        [
            jnp.zeros((groups, 1), jnp.float32),
            long_filter[:, ::-1].astype(jnp.float32),
            jnp.zeros((groups, period - span - 1), jnp.float32),
        ],
        axis=1,
    )
    return pl.pallas_call(
        toeplitz_kernel,
        out_shape=jax.ShapeDtypeStruct((groups, span, 2 * span), long_filter.dtype),
    )(row)


def line_slots(block, axis_name, size):
    index = lax.axis_index(axis_name)
    received = {}
    for offset in range(1, size):
        for d in (offset, -offset):
            pairs = [(i, i + d) for i in range(size) if 0 <= i + d < size]
            received[d] = lax.ppermute(block, axis_name, pairs)
    slots = [block]
    for k in range(1, size):
        slots.append(jnp.where(index + k < size, received[-k], received[size - k]))
    return jnp.stack(slots)


def partial_kernel(table_ref, piece_ref, weight_ref, out_ref, acc_ref):
    k = pl.program_id(0)

    @pl.when(k == 0)
    def _():
        acc_ref[...] = jnp.zeros_like(acc_ref)

    rows = weight_ref[0, :, 0]
    rows = rows.reshape(-1, rows.shape[-1])
    acc_ref[...] += jnp.dot(piece_ref[0], rows, preferred_element_type=jnp.float32)

    @pl.when(k == pl.num_programs(0) - 1)
    def _():
        out_ref[...] = acc_ref[...]


def final_kernel(table_ref, piece_ref, weight_ref, carry_ref, out_ref, acc_ref):
    k = pl.program_id(0)

    @pl.when(k == 0)
    def _():
        acc_ref[...] = carry_ref[...]

    rows = weight_ref[0, :, 0]
    rows = rows.reshape(-1, rows.shape[-1])
    acc_ref[...] += jnp.dot(piece_ref[0], rows, preferred_element_type=jnp.float32)

    @pl.when(k == pl.num_programs(0) - 1)
    def _():
        out_ref[...] = acc_ref[...].astype(out_ref.dtype)


def block_matmul(table, pieces, weight, carry=None):
    n, tok, width = pieces.shape
    _, ys, _, rows, cols = weight.shape
    in_specs = [
        pl.BlockSpec((1, tok, width), lambda k, t: (k, 0, 0)),
        pl.BlockSpec((1, ys, 1, rows, cols), lambda k, t: (t[0, k], 0, t[1, k], 0, 0)),
    ]
    args = [table, pieces, weight]
    if carry is None:
        kernel, out_dtype = partial_kernel, jnp.float32
    else:
        kernel, out_dtype = final_kernel, jnp.bfloat16
        in_specs.append(pl.BlockSpec((tok, cols), lambda k, t: (0, 0)))
        args.append(carry)
    grid_spec = pltpu.PrefetchScalarGridSpec(
        num_scalar_prefetch=1,
        grid=(n,),
        in_specs=in_specs,
        out_specs=pl.BlockSpec((tok, cols), lambda k, t: (0, 0)),
        scratch_shapes=[pltpu.VMEM((tok, cols), jnp.float32)],
    )
    return pl.pallas_call(
        kernel,
        grid_spec=grid_spec,
        out_shape=jax.ShapeDtypeStruct((tok, cols), out_dtype),
    )(*args)


def on_device(projected, short_filter, long_filter, out_weight):
    tok_rows = projected.shape[0]
    groups, span = long_filter.shape
    channels = projected.shape[2]

    partner = lax.ppermute(out_weight, "zh", [(0, 1), (1, 0)])
    zh = lax.axis_index("zh")
    pair = jnp.where(zh == 0, jnp.stack([out_weight, partner]), jnp.stack([partner, out_weight]))
    weight_xy = lax.all_gather(pair, ("x", "y"), axis=0, tiled=False)

    kv_tail = projected[tok_rows - span - 2 :, 1:]
    q_tail = projected[tok_rows - 2 :, 0][None]
    received = from_behind(jnp.concatenate([kv_tail, q_tail], axis=0))
    kv = jnp.concatenate([received[: span + 2], projected[:, 1:]], axis=0).astype(jnp.float32)
    f_kv = short_filter[0, 1:] * kv[2:] + short_filter[1, 1:] * kv[1:-1] + short_filter[2, 1:] * kv[:-2]
    product = (f_kv[:, 0] * f_kv[:, 1]).astype(jnp.bfloat16)
    q = jnp.concatenate([received[span + 2], projected[:, 0]], axis=0).astype(jnp.float32)
    query = short_filter[0, 0] * q[2:] + short_filter[1, 0] * q[1:-1] + short_filter[2, 0] * q[:-2]

    blocks = product.reshape(tok_rows // span + 1, span, groups, channels // groups)
    window = jnp.concatenate([blocks[:-1], blocks[1:]], axis=1)
    toeplitz = toeplitz_blocks(long_filter)
    filtered = jnp.einsum(
        "gij,bjgc->bigc", toeplitz, window, preferred_element_type=jnp.float32
    ).reshape(tok_rows, channels)
    gated = (query * filtered).astype(jnp.bfloat16)

    own = line_slots(gated, "zl", 4)
    other = lax.ppermute(own, "c", [(0, 1), (1, 0)])
    zl = lax.axis_index("zl")
    core = lax.axis_index("c")
    blocks = jnp.concatenate([own, other])
    order = []
    for w in range(8):
        slot = (w // 2 - zl) % 4
        order.append(jnp.where(w % 2 == core, slot, 4 + slot))
    by_w = jnp.take(blocks, jnp.stack(order), axis=0, mode="clip")
    g5 = by_w.reshape(2, 4, tok_rows, 8, -1)
    w5 = weight_xy.reshape(4, 8, 2, g5.shape[-1], -1)
    mixed = jnp.einsum("zxtyr,xyzro->to", g5, w5, preferred_element_type=jnp.float32)
    return mixed.astype(jnp.bfloat16)


def solution(mesh):
    names = SEQ + WIDTH
    sizes = tuple(s for _, s in SEQ_PARTS + WIDTH_PARTS)
    fine = Mesh(mesh.devices.reshape(sizes), names)
    in_specs = (
        P(SEQ, None, WIDTH),
        P(None, None, WIDTH),
        P(WIDTH, None),
        P(SEQ, WIDTH),
    )
    out_specs = P(SEQ, WIDTH)
    return jax.shard_map(
        on_device, mesh=fine, in_specs=in_specs, out_specs=out_specs, check_vma=False
    )
```

```python
import jax
import jax.numpy as jnp
from jax import lax
from jax.experimental import pallas as pl
from jax.experimental.pallas import tpu as pltpu
from jax.sharding import Mesh
from jax.sharding import PartitionSpec as P

SEQ_PARTS = (("zh", 2), ("x", 4), ("y", 8))
WIDTH_PARTS = (("zl", 4), ("c", 2))
SEQ = tuple(n for n, _ in SEQ_PARTS)
WIDTH = tuple(n for n, _ in WIDTH_PARTS)


def from_behind(array):
    total = 1
    for _, size in SEQ_PARTS:
        total *= size
    pairs = [(i, i + 1) for i in range(total - 1)]
    return lax.ppermute(array, SEQ, pairs)


def toeplitz_kernel(row_ref, out_ref):
    groups, span, width = out_ref.shape
    period = row_ref.shape[1]

    def one_group(g, carry):
        row = row_ref[pl.ds(g, 1), :]
        tiled = jnp.broadcast_to(row, (span, period))
        rolled = pltpu.roll(tiled, shift=0, axis=1, stride=1, stride_axis=0)
        out_ref[g] = rolled[:, :width].astype(out_ref.dtype)
        return carry

    lax.fori_loop(0, groups, one_group, 0)


def toeplitz_blocks(long_filter):
    groups, span = long_filter.shape
    period = 3 * span
    row = jnp.concatenate(
        [
            jnp.zeros((groups, 1), jnp.float32),
            long_filter[:, ::-1].astype(jnp.float32),
            jnp.zeros((groups, period - span - 1), jnp.float32),
        ],
        axis=1,
    )
    return pl.pallas_call(
        toeplitz_kernel,
        out_shape=jax.ShapeDtypeStruct((groups, span, 2 * span), long_filter.dtype),
    )(row)


def line_slots(block, axis_name, size):
    index = lax.axis_index(axis_name)
    received = {}
    for offset in range(1, size):
        for d in (offset, -offset):
            pairs = [(i, i + d) for i in range(size) if 0 <= i + d < size]
            received[d] = lax.ppermute(block, axis_name, pairs)
    slots = [block]
    for k in range(1, size):
        slots.append(jnp.where(index + k < size, received[-k], received[size - k]))
    return jnp.stack(slots)


def ring_gather(piece, axis_name, size, absolute=True):
    index = lax.axis_index(axis_name)
    right = [(i, (i + 1) % size) for i in range(size)]
    left = [(i, (i - 1) % size) for i in range(size)]
    relative = [None] * size
    relative[0] = piece
    from_left = piece
    from_right = piece
    for step in range(1, size // 2 + 1):
        from_left = lax.ppermute(from_left, axis_name, right)
        relative[(size - step) % size] = from_left
        if step < size - step:
            from_right = lax.ppermute(from_right, axis_name, left)
            relative[step] = from_right
    if not absolute:
        return jnp.stack(relative)
    stacked = jnp.stack(relative + relative)
    return lax.dynamic_slice_in_dim(stacked, (size - index) % size, size, axis=0)


def partial_kernel(table_ref, piece_ref, weight_ref, out_ref, acc_ref):
    k = pl.program_id(0)

    @pl.when(k == 0)
    def _():
        acc_ref[...] = jnp.zeros_like(acc_ref)

    rows = weight_ref[0, :, 0]
    rows = rows.reshape(-1, rows.shape[-1])
    acc_ref[...] += jnp.dot(piece_ref[0], rows, preferred_element_type=jnp.float32)

    @pl.when(k == pl.num_programs(0) - 1)
    def _():
        out_ref[...] = acc_ref[...]


def final_kernel(table_ref, piece_ref, weight_ref, carry_ref, out_ref, acc_ref):
    k = pl.program_id(0)

    @pl.when(k == 0)
    def _():
        acc_ref[...] = carry_ref[...]

    rows = weight_ref[0, :, 0]
    rows = rows.reshape(-1, rows.shape[-1])
    acc_ref[...] += jnp.dot(piece_ref[0], rows, preferred_element_type=jnp.float32)

    @pl.when(k == pl.num_programs(0) - 1)
    def _():
        out_ref[...] = acc_ref[...].astype(out_ref.dtype)


def block_matmul(table, pieces, weight, carry=None):
    n, tok, width = pieces.shape
    _, ys, _, rows, cols = weight.shape
    in_specs = [
        pl.BlockSpec((1, tok, width), lambda k, t: (k, 0, 0)),
        pl.BlockSpec((1, ys, 1, rows, cols), lambda k, t: (t[0, k], 0, t[1, k], 0, 0)),
    ]
    args = [table, pieces, weight]
    if carry is None:
        kernel, out_dtype = partial_kernel, jnp.float32
    else:
        kernel, out_dtype = final_kernel, jnp.bfloat16
        in_specs.append(pl.BlockSpec((tok, cols), lambda k, t: (0, 0)))
        args.append(carry)
    grid_spec = pltpu.PrefetchScalarGridSpec(
        num_scalar_prefetch=1,
        grid=(n,),
        in_specs=in_specs,
        out_specs=pl.BlockSpec((tok, cols), lambda k, t: (0, 0)),
        scratch_shapes=[pltpu.VMEM((tok, cols), jnp.float32)],
    )
    return pl.pallas_call(
        kernel,
        grid_spec=grid_spec,
        out_shape=jax.ShapeDtypeStruct((tok, cols), out_dtype),
    )(*args)


def on_device(projected, short_filter, long_filter, out_weight):
    tok_rows = projected.shape[0]
    groups, span = long_filter.shape
    channels = projected.shape[2]

    partner = lax.ppermute(out_weight, "zh", [(0, 1), (1, 0)])
    zh = lax.axis_index("zh")
    pair = jnp.where(zh == 0, jnp.stack([out_weight, partner]), jnp.stack([partner, out_weight]))
    weight_y = ring_gather(pair, "y", 8)
    weight_xy = ring_gather(weight_y, "x", 4, absolute=False)

    kv_tail = projected[tok_rows - span - 2 :, 1:]
    q_tail = projected[tok_rows - 2 :, 0][None]
    received = from_behind(jnp.concatenate([kv_tail, q_tail], axis=0))
    kv = jnp.concatenate([received[: span + 2], projected[:, 1:]], axis=0).astype(jnp.float32)
    f_kv = short_filter[0, 1:] * kv[2:] + short_filter[1, 1:] * kv[1:-1] + short_filter[2, 1:] * kv[:-2]
    product = (f_kv[:, 0] * f_kv[:, 1]).astype(jnp.bfloat16)
    q = jnp.concatenate([received[span + 2], projected[:, 0]], axis=0).astype(jnp.float32)
    query = short_filter[0, 0] * q[2:] + short_filter[1, 0] * q[1:-1] + short_filter[2, 0] * q[:-2]

    blocks = product.reshape(tok_rows // span + 1, span, groups, channels // groups)
    window = jnp.concatenate([blocks[:-1], blocks[1:]], axis=1)
    toeplitz = toeplitz_blocks(long_filter)
    filtered = jnp.einsum(
        "gij,bjgc->bigc", toeplitz, window, preferred_element_type=jnp.float32
    ).reshape(tok_rows, channels)
    gated = (query * filtered).astype(jnp.bfloat16)

    own = line_slots(gated, "zl", 4)
    other = lax.ppermute(own, "c", [(0, 1), (1, 0)])
    zl = lax.axis_index("zl")
    core = lax.axis_index("c")
    sources = (zl + jnp.arange(4, dtype=jnp.int32)) % 4

    def table_for(c):
        w = 2 * sources + c
        return jnp.stack([(w - lax.axis_index("x")) % 4, w // 4]).astype(jnp.int32)

    carry = block_matmul(table_for(core), own, weight_xy)
    return block_matmul(table_for(1 - core), other, weight_xy, carry)


def solution(mesh):
    names = SEQ + WIDTH
    sizes = tuple(s for _, s in SEQ_PARTS + WIDTH_PARTS)
    fine = Mesh(mesh.devices.reshape(sizes), names)
    in_specs = (
        P(SEQ, None, WIDTH),
        P(None, None, WIDTH),
        P(WIDTH, None),
        P(SEQ, WIDTH),
    )
    out_specs = P(SEQ, WIDTH)
    return jax.shard_map(
        on_device, mesh=fine, in_specs=in_specs, out_specs=out_specs, check_vma=False
    )
```

```python
import jax
import jax.numpy as jnp
from jax import lax
from jax.experimental import pallas as pl
from jax.experimental.pallas import tpu as pltpu
from jax.sharding import Mesh
from jax.sharding import PartitionSpec as P

SEQ_PARTS = (("zh", 2), ("x", 4), ("y", 8))
WIDTH_PARTS = (("zl", 4), ("c", 2))
SEQ = tuple(n for n, _ in SEQ_PARTS)
WIDTH = tuple(n for n, _ in WIDTH_PARTS)


def from_behind(array):
    total = 1
    for _, size in SEQ_PARTS:
        total *= size
    pairs = [(i, i + 1) for i in range(total - 1)]
    return lax.ppermute(array, SEQ, pairs)


def toeplitz_kernel(row_ref, out_ref):
    groups, span, width = out_ref.shape
    period = row_ref.shape[1]

    def one_group(g, carry):
        row = row_ref[pl.ds(g, 1), :]
        tiled = jnp.broadcast_to(row, (span, period))
        rolled = pltpu.roll(tiled, shift=0, axis=1, stride=1, stride_axis=0)
        out_ref[g] = rolled[:, :width].astype(out_ref.dtype)
        return carry

    lax.fori_loop(0, groups, one_group, 0)


def toeplitz_blocks(long_filter):
    groups, span = long_filter.shape
    period = 3 * span
    row = jnp.concatenate(
        [
            jnp.zeros((groups, 1), jnp.float32),
            long_filter[:, ::-1].astype(jnp.float32),
            jnp.zeros((groups, period - span - 1), jnp.float32),
        ],
        axis=1,
    )
    return pl.pallas_call(
        toeplitz_kernel,
        out_shape=jax.ShapeDtypeStruct((groups, span, 2 * span), long_filter.dtype),
    )(row)


def line_slots(block, axis_name, size):
    index = lax.axis_index(axis_name)
    received = {}
    for offset in range(1, size):
        for d in (offset, -offset):
            pairs = [(i, i + d) for i in range(size) if 0 <= i + d < size]
            received[d] = lax.ppermute(block, axis_name, pairs)
    slots = [block]
    for k in range(1, size):
        slots.append(jnp.where(index + k < size, received[-k], received[size - k]))
    return jnp.stack(slots)


def partial_kernel(table_ref, piece_ref, weight_ref, out_ref, acc_ref):
    k = pl.program_id(0)

    @pl.when(k == 0)
    def _():
        acc_ref[...] = jnp.zeros_like(acc_ref)

    rows = weight_ref[0, :, 0]
    rows = rows.reshape(-1, rows.shape[-1])
    acc_ref[...] += jnp.dot(piece_ref[0], rows, preferred_element_type=jnp.float32)

    @pl.when(k == pl.num_programs(0) - 1)
    def _():
        out_ref[...] = acc_ref[...]


def final_kernel(table_ref, piece_ref, weight_ref, carry_ref, out_ref, acc_ref):
    k = pl.program_id(0)

    @pl.when(k == 0)
    def _():
        acc_ref[...] = carry_ref[...]

    rows = weight_ref[0, :, 0]
    rows = rows.reshape(-1, rows.shape[-1])
    acc_ref[...] += jnp.dot(piece_ref[0], rows, preferred_element_type=jnp.float32)

    @pl.when(k == pl.num_programs(0) - 1)
    def _():
        out_ref[...] = acc_ref[...].astype(out_ref.dtype)


def block_matmul(table, pieces, weight, carry=None):
    n, tok, width = pieces.shape
    _, ys, _, rows, cols = weight.shape
    in_specs = [
        pl.BlockSpec((1, tok, width), lambda k, t: (k, 0, 0)),
        pl.BlockSpec((1, ys, 1, rows, cols), lambda k, t: (t[0, k], 0, t[1, k], 0, 0)),
    ]
    args = [table, pieces, weight]
    if carry is None:
        kernel, out_dtype = partial_kernel, jnp.float32
    else:
        kernel, out_dtype = final_kernel, jnp.bfloat16
        in_specs.append(pl.BlockSpec((tok, cols), lambda k, t: (0, 0)))
        args.append(carry)
    grid_spec = pltpu.PrefetchScalarGridSpec(
        num_scalar_prefetch=1,
        grid=(n,),
        in_specs=in_specs,
        out_specs=pl.BlockSpec((tok, cols), lambda k, t: (0, 0)),
        scratch_shapes=[pltpu.VMEM((tok, cols), jnp.float32)],
    )
    return pl.pallas_call(
        kernel,
        grid_spec=grid_spec,
        out_shape=jax.ShapeDtypeStruct((tok, cols), out_dtype),
    )(*args)


def on_device(projected, short_filter, long_filter, out_weight):
    tok_rows = projected.shape[0]
    groups, span = long_filter.shape
    channels = projected.shape[2]

    partner = lax.ppermute(out_weight, "zh", [(0, 1), (1, 0)])
    zh = lax.axis_index("zh")
    pair = jnp.stack([out_weight, partner])
    weight_xy = lax.all_gather(pair, ("x", "y"), axis=0, tiled=False)

    kv_tail = projected[tok_rows - span - 2 :, 1:]
    q_tail = projected[tok_rows - 2 :, 0][None]
    received = from_behind(jnp.concatenate([kv_tail, q_tail], axis=0))
    kv = jnp.concatenate([received[: span + 2], projected[:, 1:]], axis=0).astype(jnp.float32)
    f_kv = short_filter[0, 1:] * kv[2:] + short_filter[1, 1:] * kv[1:-1] + short_filter[2, 1:] * kv[:-2]
    product = (f_kv[:, 0] * f_kv[:, 1]).astype(jnp.bfloat16)
    q = jnp.concatenate([received[span + 2], projected[:, 0]], axis=0).astype(jnp.float32)
    query = short_filter[0, 0] * q[2:] + short_filter[1, 0] * q[1:-1] + short_filter[2, 0] * q[:-2]

    blocks = product.reshape(tok_rows // span + 1, span, groups, channels // groups)
    window = jnp.concatenate([blocks[:-1], blocks[1:]], axis=1)
    toeplitz = toeplitz_blocks(long_filter)
    filtered = jnp.einsum(
        "gij,bjgc->bigc", toeplitz, window, preferred_element_type=jnp.float32
    ).reshape(tok_rows, channels)
    gated = (query * filtered).astype(jnp.bfloat16)

    own = line_slots(gated, "zl", 4)
    other = lax.ppermute(own, "c", [(0, 1), (1, 0)])
    zl = lax.axis_index("zl")
    core = lax.axis_index("c")
    sources = (zl + jnp.arange(4, dtype=jnp.int32)) % 4

    def table_for(c):
        w = 2 * sources + c
        return jnp.stack([w % 4, (w // 4 + zh) % 2]).astype(jnp.int32)

    weight = weight_xy.reshape(4, 8, *weight_xy.shape[1:])
    carry = block_matmul(table_for(core), own, weight)
    return block_matmul(table_for(1 - core), other, weight, carry)


def solution(mesh):
    names = SEQ + WIDTH
    sizes = tuple(s for _, s in SEQ_PARTS + WIDTH_PARTS)
    fine = Mesh(mesh.devices.reshape(sizes), names)
    in_specs = (
        P(SEQ, None, WIDTH),
        P(None, None, WIDTH),
        P(WIDTH, None),
        P(SEQ, WIDTH),
    )
    out_specs = P(SEQ, WIDTH)
    return jax.shard_map(
        on_device, mesh=fine, in_specs=in_specs, out_specs=out_specs, check_vma=False
    )
```

```python
import jax
import jax.numpy as jnp
from jax import lax
from jax.experimental import pallas as pl
from jax.experimental.pallas import tpu as pltpu
from jax.sharding import Mesh
from jax.sharding import PartitionSpec as P

SEQ_PARTS = (("zh", 2), ("x", 4), ("y", 8))
WIDTH_PARTS = (("zl", 4), ("c", 2))
SEQ = tuple(n for n, _ in SEQ_PARTS)
WIDTH = tuple(n for n, _ in WIDTH_PARTS)


def from_behind(array):
    total = 1
    for _, size in SEQ_PARTS:
        total *= size
    pairs = [(i, i + 1) for i in range(total - 1)]
    return lax.ppermute(array, SEQ, pairs)


def toeplitz_kernel(row_ref, out_ref):
    groups, span, width = out_ref.shape
    period = row_ref.shape[1]

    def one_group(g, carry):
        row = row_ref[pl.ds(g, 1), :]
        tiled = jnp.broadcast_to(row, (span, period))
        rolled = pltpu.roll(tiled, shift=0, axis=1, stride=1, stride_axis=0)
        out_ref[g] = rolled[:, :width].astype(out_ref.dtype)
        return carry

    lax.fori_loop(0, groups, one_group, 0)


def toeplitz_blocks(long_filter):
    groups, span = long_filter.shape
    period = 3 * span
    row = jnp.concatenate(
        [
            jnp.zeros((groups, 1), jnp.float32),
            long_filter[:, ::-1].astype(jnp.float32),
            jnp.zeros((groups, period - span - 1), jnp.float32),
        ],
        axis=1,
    )
    return pl.pallas_call(
        toeplitz_kernel,
        out_shape=jax.ShapeDtypeStruct((groups, span, 2 * span), long_filter.dtype),
    )(row)


def line_slots(block, axis_name, size):
    index = lax.axis_index(axis_name)
    received = {}
    for offset in range(1, size):
        for d in (offset, -offset):
            pairs = [(i, i + d) for i in range(size) if 0 <= i + d < size]
            received[d] = lax.ppermute(block, axis_name, pairs)
    slots = [block]
    for k in range(1, size):
        slots.append(jnp.where(index + k < size, received[-k], received[size - k]))
    return jnp.stack(slots)


def partial_kernel(table_ref, piece_ref, weight_a_ref, weight_b_ref, out_ref, acc_ref):
    k = pl.program_id(0)

    @pl.when(k == 0)
    def _():
        acc_ref[...] = jnp.zeros_like(acc_ref)

    acc_ref[...] += two_blocks(piece_ref, weight_a_ref, weight_b_ref)

    @pl.when(k == pl.num_programs(0) - 1)
    def _():
        out_ref[...] = acc_ref[...]


def final_kernel(table_ref, piece_ref, weight_a_ref, weight_b_ref, carry_ref, out_ref, acc_ref):
    k = pl.program_id(0)

    @pl.when(k == 0)
    def _():
        acc_ref[...] = carry_ref[...]

    acc_ref[...] += two_blocks(piece_ref, weight_a_ref, weight_b_ref)

    @pl.when(k == pl.num_programs(0) - 1)
    def _():
        out_ref[...] = acc_ref[...].astype(out_ref.dtype)


def two_blocks(piece_ref, weight_a_ref, weight_b_ref):
    rows_a = weight_a_ref[0, :, 0]
    rows_b = weight_b_ref[0, :, 0]
    rows_a = rows_a.reshape(-1, rows_a.shape[-1])
    rows_b = rows_b.reshape(-1, rows_b.shape[-1])
    total = jnp.dot(piece_ref[0], rows_a, preferred_element_type=jnp.float32)
    return total + jnp.dot(piece_ref[1], rows_b, preferred_element_type=jnp.float32)


def block_matmul(table, pieces, weight, carry=None):
    n, tok, width = pieces.shape
    _, ys, _, rows, cols = weight.shape
    in_specs = [
        pl.BlockSpec((2, tok, width), lambda k, t: (k, 0, 0)),
        pl.BlockSpec((1, ys, 1, rows, cols), lambda k, t: (t[0, 2 * k], 0, t[1, 2 * k], 0, 0)),
        pl.BlockSpec((1, ys, 1, rows, cols), lambda k, t: (t[0, 2 * k + 1], 0, t[1, 2 * k + 1], 0, 0)),
    ]
    args = [table, pieces, weight, weight]
    if carry is None:
        kernel, out_dtype = partial_kernel, jnp.float32
    else:
        kernel, out_dtype = final_kernel, jnp.bfloat16
        in_specs.append(pl.BlockSpec((tok, cols), lambda k, t: (0, 0)))
        args.append(carry)
    grid_spec = pltpu.PrefetchScalarGridSpec(
        num_scalar_prefetch=1,
        grid=(n // 2,),
        in_specs=in_specs,
        out_specs=pl.BlockSpec((tok, cols), lambda k, t: (0, 0)),
        scratch_shapes=[pltpu.VMEM((tok, cols), jnp.float32)],
    )
    return pl.pallas_call(
        kernel,
        grid_spec=grid_spec,
        out_shape=jax.ShapeDtypeStruct((tok, cols), out_dtype),
    )(*args)


def on_device(projected, short_filter, long_filter, out_weight):
    tok_rows = projected.shape[0]
    groups, span = long_filter.shape
    channels = projected.shape[2]

    partner = lax.ppermute(out_weight, "zh", [(0, 1), (1, 0)])
    zh = lax.axis_index("zh")
    pair = jnp.stack([out_weight, partner])
    weight_xy = lax.all_gather(pair, ("x", "y"), axis=0, tiled=False)

    kv_tail = projected[tok_rows - span - 2 :, 1:]
    q_tail = projected[tok_rows - 2 :, 0][None]
    received = from_behind(jnp.concatenate([kv_tail, q_tail], axis=0))
    kv = jnp.concatenate([received[: span + 2], projected[:, 1:]], axis=0).astype(jnp.float32)
    f_kv = short_filter[0, 1:] * kv[2:] + short_filter[1, 1:] * kv[1:-1] + short_filter[2, 1:] * kv[:-2]
    product = (f_kv[:, 0] * f_kv[:, 1]).astype(jnp.bfloat16)
    q = jnp.concatenate([received[span + 2], projected[:, 0]], axis=0).astype(jnp.float32)
    query = short_filter[0, 0] * q[2:] + short_filter[1, 0] * q[1:-1] + short_filter[2, 0] * q[:-2]

    blocks = product.reshape(tok_rows // span + 1, span, groups, channels // groups)
    window = jnp.concatenate([blocks[:-1], blocks[1:]], axis=1)
    toeplitz = toeplitz_blocks(long_filter)
    filtered = jnp.einsum(
        "gij,bjgc->bigc", toeplitz, window, preferred_element_type=jnp.float32
    ).reshape(tok_rows, channels)
    gated = (query * filtered).astype(jnp.bfloat16)

    own = line_slots(gated, "zl", 4)
    other = lax.ppermute(own, "c", [(0, 1), (1, 0)])
    zl = lax.axis_index("zl")
    core = lax.axis_index("c")
    sources = (zl + jnp.arange(4, dtype=jnp.int32)) % 4

    def table_for(c):
        w = 2 * sources + c
        return jnp.stack([w % 4, (w // 4 + zh) % 2]).astype(jnp.int32)

    weight = weight_xy.reshape(4, 8, *weight_xy.shape[1:])
    carry = block_matmul(table_for(core), own, weight)
    return block_matmul(table_for(1 - core), other, weight, carry)


def solution(mesh):
    names = SEQ + WIDTH
    sizes = tuple(s for _, s in SEQ_PARTS + WIDTH_PARTS)
    fine = Mesh(mesh.devices.reshape(sizes), names)
    in_specs = (
        P(SEQ, None, WIDTH),
        P(None, None, WIDTH),
        P(WIDTH, None),
        P(SEQ, WIDTH),
    )
    out_specs = P(SEQ, WIDTH)
    return jax.shard_map(
        on_device, mesh=fine, in_specs=in_specs, out_specs=out_specs, check_vma=False
    )
```

```python
import jax
import jax.numpy as jnp
from jax import lax
from jax.experimental import pallas as pl
from jax.experimental.pallas import tpu as pltpu
from jax.sharding import Mesh
from jax.sharding import PartitionSpec as P

SEQ_PARTS = (("zh", 2), ("x", 4), ("y", 8))
WIDTH_PARTS = (("zl", 4), ("c", 2))
SEQ = tuple(n for n, _ in SEQ_PARTS)
WIDTH = tuple(n for n, _ in WIDTH_PARTS)


def from_behind(array):
    total = 1
    for _, size in SEQ_PARTS:
        total *= size
    pairs = [(i, i + 1) for i in range(total - 1)]
    return lax.ppermute(array, SEQ, pairs)


def toeplitz_kernel(row_ref, out_ref):
    groups, span, width = out_ref.shape
    period = row_ref.shape[1]

    def one_group(g, carry):
        row = row_ref[pl.ds(g, 1), :]
        tiled = jnp.broadcast_to(row, (span, period))
        rolled = pltpu.roll(tiled, shift=0, axis=1, stride=1, stride_axis=0)
        out_ref[g] = rolled[:, :width].astype(out_ref.dtype)
        return carry

    lax.fori_loop(0, groups, one_group, 0)


def toeplitz_blocks(long_filter):
    groups, span = long_filter.shape
    period = 3 * span
    row = jnp.concatenate(
        [
            jnp.zeros((groups, 1), jnp.float32),
            long_filter[:, ::-1].astype(jnp.float32),
            jnp.zeros((groups, period - span - 1), jnp.float32),
        ],
        axis=1,
    )
    return pl.pallas_call(
        toeplitz_kernel,
        out_shape=jax.ShapeDtypeStruct((groups, span, 2 * span), long_filter.dtype),
    )(row)


def line_slots(block, axis_name, size):
    index = lax.axis_index(axis_name)
    received = {}
    for offset in range(1, size):
        for d in (offset, -offset):
            pairs = [(i, i + d) for i in range(size) if 0 <= i + d < size]
            received[d] = lax.ppermute(block, axis_name, pairs)
    slots = [block]
    for k in range(1, size):
        slots.append(jnp.where(index + k < size, received[-k], received[size - k]))
    return jnp.stack(slots)


def matmul_kernel(table_ref, own_ref, other_ref, weight_a_ref, weight_b_ref, out_ref, acc_ref):
    k = pl.program_id(0)
    half = pl.num_programs(0) // 2

    @pl.when(k == 0)
    def _():
        acc_ref[...] = jnp.zeros_like(acc_ref)

    @pl.when(k < half)
    def _():
        acc_ref[...] += two_blocks(own_ref, weight_a_ref, weight_b_ref)

    @pl.when(k >= half)
    def _():
        acc_ref[...] += two_blocks(other_ref, weight_a_ref, weight_b_ref)

    @pl.when(k == pl.num_programs(0) - 1)
    def _():
        out_ref[...] = acc_ref[...].astype(out_ref.dtype)


def two_blocks(piece_ref, weight_a_ref, weight_b_ref):
    rows_a = weight_a_ref[0, :, 0]
    rows_b = weight_b_ref[0, :, 0]
    rows_a = rows_a.reshape(-1, rows_a.shape[-1])
    rows_b = rows_b.reshape(-1, rows_b.shape[-1])
    total = jnp.dot(piece_ref[0], rows_a, preferred_element_type=jnp.float32)
    return total + jnp.dot(piece_ref[1], rows_b, preferred_element_type=jnp.float32)


def block_matmul(table, own, other, weight):
    n, tok, width = own.shape
    _, ys, _, rows, cols = weight.shape
    steps = n // 2
    in_specs = [
        pl.BlockSpec((2, tok, width), lambda k, t: (jnp.minimum(k, steps - 1), 0, 0)),
        pl.BlockSpec((2, tok, width), lambda k, t: (jnp.maximum(k - steps, 0), 0, 0)),
        pl.BlockSpec((1, ys, 1, rows, cols), lambda k, t: (t[0, 2 * k], 0, t[1, 2 * k], 0, 0)),
        pl.BlockSpec((1, ys, 1, rows, cols), lambda k, t: (t[0, 2 * k + 1], 0, t[1, 2 * k + 1], 0, 0)),
    ]
    grid_spec = pltpu.PrefetchScalarGridSpec(
        num_scalar_prefetch=1,
        grid=(2 * steps,),
        in_specs=in_specs,
        out_specs=pl.BlockSpec((tok, cols), lambda k, t: (0, 0)),
        scratch_shapes=[pltpu.VMEM((tok, cols), jnp.float32)],
    )
    return pl.pallas_call(
        matmul_kernel,
        grid_spec=grid_spec,
        out_shape=jax.ShapeDtypeStruct((tok, cols), jnp.bfloat16),
    )(table, own, other, weight, weight)


def on_device(projected, short_filter, long_filter, out_weight):
    tok_rows = projected.shape[0]
    groups, span = long_filter.shape
    channels = projected.shape[2]

    partner = lax.ppermute(out_weight, "zh", [(0, 1), (1, 0)])
    zh = lax.axis_index("zh")
    pair = jnp.stack([out_weight, partner])
    weight_xy = lax.all_gather(pair, ("x", "y"), axis=0, tiled=False)

    kv_tail = projected[tok_rows - span - 2 :, 1:]
    q_tail = projected[tok_rows - 2 :, 0][None]
    received = from_behind(jnp.concatenate([kv_tail, q_tail], axis=0))
    kv = jnp.concatenate([received[: span + 2], projected[:, 1:]], axis=0).astype(jnp.float32)
    f_kv = short_filter[0, 1:] * kv[2:] + short_filter[1, 1:] * kv[1:-1] + short_filter[2, 1:] * kv[:-2]
    product = (f_kv[:, 0] * f_kv[:, 1]).astype(jnp.bfloat16)
    q = jnp.concatenate([received[span + 2], projected[:, 0]], axis=0).astype(jnp.float32)
    query = short_filter[0, 0] * q[2:] + short_filter[1, 0] * q[1:-1] + short_filter[2, 0] * q[:-2]

    blocks = product.reshape(tok_rows // span + 1, span, groups, channels // groups)
    window = jnp.concatenate([blocks[:-1], blocks[1:]], axis=1)
    toeplitz = toeplitz_blocks(long_filter)
    filtered = jnp.einsum(
        "gij,bjgc->bigc", toeplitz, window, preferred_element_type=jnp.float32
    ).reshape(tok_rows, channels)
    gated = (query * filtered).astype(jnp.bfloat16)

    own = line_slots(gated, "zl", 4)
    other = lax.ppermute(own, "c", [(0, 1), (1, 0)])
    zl = lax.axis_index("zl")
    core = lax.axis_index("c")
    sources = (zl + jnp.arange(4, dtype=jnp.int32)) % 4

    def table_for(c):
        w = 2 * sources + c
        return jnp.stack([w % 4, (w // 4 + zh) % 2]).astype(jnp.int32)

    weight = weight_xy.reshape(4, 8, *weight_xy.shape[1:])
    table = jnp.concatenate([table_for(core), table_for(1 - core)], axis=1)
    return block_matmul(table, own, other, weight)


def solution(mesh):
    names = SEQ + WIDTH
    sizes = tuple(s for _, s in SEQ_PARTS + WIDTH_PARTS)
    fine = Mesh(mesh.devices.reshape(sizes), names)
    in_specs = (
        P(SEQ, None, WIDTH),
        P(None, None, WIDTH),
        P(WIDTH, None),
        P(SEQ, WIDTH),
    )
    out_specs = P(SEQ, WIDTH)
    return jax.shard_map(
        on_device, mesh=fine, in_specs=in_specs, out_specs=out_specs, check_vma=False
    )
```

```python
import jax
import jax.numpy as jnp
from jax import lax
from jax.experimental import pallas as pl
from jax.experimental.pallas import tpu as pltpu
from jax.sharding import Mesh
from jax.sharding import PartitionSpec as P

SEQ_PARTS = (("zh", 2), ("x", 4), ("y", 8))
WIDTH_PARTS = (("zl", 4), ("c", 2))
SEQ = tuple(n for n, _ in SEQ_PARTS)
WIDTH = tuple(n for n, _ in WIDTH_PARTS)


def from_behind(array):
    total = 1
    for _, size in SEQ_PARTS:
        total *= size
    pairs = [(i, i + 1) for i in range(total - 1)]
    return lax.ppermute(array, SEQ, pairs)


def toeplitz_kernel(row_ref, out_ref):
    groups, span, width = out_ref.shape
    period = row_ref.shape[1]

    def one_group(g, carry):
        row = row_ref[pl.ds(g, 1), :]
        tiled = jnp.broadcast_to(row, (span, period))
        rolled = pltpu.roll(tiled, shift=0, axis=1, stride=1, stride_axis=0)
        out_ref[g] = rolled[:, :width].astype(out_ref.dtype)
        return carry

    lax.fori_loop(0, groups, one_group, 0)


def toeplitz_blocks(long_filter):
    groups, span = long_filter.shape
    period = 3 * span
    row = jnp.concatenate(
        [
            jnp.zeros((groups, 1), jnp.float32),
            long_filter[:, ::-1].astype(jnp.float32),
            jnp.zeros((groups, period - span - 1), jnp.float32),
        ],
        axis=1,
    )
    return pl.pallas_call(
        toeplitz_kernel,
        out_shape=jax.ShapeDtypeStruct((groups, span, 2 * span), long_filter.dtype),
    )(row)


def line_slots(block, axis_name, size):
    index = lax.axis_index(axis_name)
    received = {}
    for offset in range(1, size):
        for d in (offset, -offset):
            pairs = [(i, i + d) for i in range(size) if 0 <= i + d < size]
            received[d] = lax.ppermute(block, axis_name, pairs)
    slots = [block]
    for k in range(1, size):
        slots.append(jnp.where(index + k < size, received[-k], received[size - k]))
    return jnp.stack(slots, axis=1).reshape(block.shape[0], -1)


def matmul_kernel(table_ref, own_ref, other_ref, weight_a_ref, weight_b_ref, out_ref, acc_ref):
    k = pl.program_id(0)
    half = pl.num_programs(0) // 2

    @pl.when(k == 0)
    def _():
        acc_ref[...] = jnp.zeros_like(acc_ref)

    @pl.when(k < half)
    def _():
        acc_ref[...] += two_blocks(own_ref, weight_a_ref, weight_b_ref)

    @pl.when(k >= half)
    def _():
        acc_ref[...] += two_blocks(other_ref, weight_a_ref, weight_b_ref)

    @pl.when(k == pl.num_programs(0) - 1)
    def _():
        out_ref[...] = acc_ref[...].astype(out_ref.dtype)


def two_blocks(piece_ref, weight_a_ref, weight_b_ref):
    rows_a = weight_a_ref[0, :, 0]
    rows_b = weight_b_ref[0, :, 0]
    rows = jnp.concatenate(
        [rows_a.reshape(-1, rows_a.shape[-1]), rows_b.reshape(-1, rows_b.shape[-1])], axis=0
    )
    return jnp.dot(piece_ref[...], rows, preferred_element_type=jnp.float32)


def block_matmul(table, own, other, weight):
    tok, total = own.shape
    _, ys, _, rows, cols = weight.shape
    width = ys * rows
    steps = total // (2 * width)
    in_specs = [
        pl.BlockSpec((tok, 2 * width), lambda k, t: (0, jnp.minimum(k, steps - 1))),
        pl.BlockSpec((tok, 2 * width), lambda k, t: (0, jnp.maximum(k - steps, 0))),
        pl.BlockSpec((1, ys, 1, rows, cols), lambda k, t: (t[0, 2 * k], 0, t[1, 2 * k], 0, 0)),
        pl.BlockSpec((1, ys, 1, rows, cols), lambda k, t: (t[0, 2 * k + 1], 0, t[1, 2 * k + 1], 0, 0)),
    ]
    grid_spec = pltpu.PrefetchScalarGridSpec(
        num_scalar_prefetch=1,
        grid=(2 * steps,),
        in_specs=in_specs,
        out_specs=pl.BlockSpec((tok, cols), lambda k, t: (0, 0)),
        scratch_shapes=[pltpu.VMEM((tok, cols), jnp.float32)],
    )
    return pl.pallas_call(
        matmul_kernel,
        grid_spec=grid_spec,
        out_shape=jax.ShapeDtypeStruct((tok, cols), jnp.bfloat16),
    )(table, own, other, weight, weight)


def on_device(projected, short_filter, long_filter, out_weight):
    tok_rows = projected.shape[0]
    groups, span = long_filter.shape
    channels = projected.shape[2]

    partner = lax.ppermute(out_weight, "zh", [(0, 1), (1, 0)])
    zh = lax.axis_index("zh")
    pair = jnp.stack([out_weight, partner])
    weight_xy = lax.all_gather(pair, ("x", "y"), axis=0, tiled=False)

    kv_tail = projected[tok_rows - span - 2 :, 1:]
    q_tail = projected[tok_rows - 2 :, 0][None]
    received = from_behind(jnp.concatenate([kv_tail, q_tail], axis=0))
    kv = jnp.concatenate([received[: span + 2], projected[:, 1:]], axis=0).astype(jnp.float32)
    f_kv = short_filter[0, 1:] * kv[2:] + short_filter[1, 1:] * kv[1:-1] + short_filter[2, 1:] * kv[:-2]
    product = (f_kv[:, 0] * f_kv[:, 1]).astype(jnp.bfloat16)
    q = jnp.concatenate([received[span + 2], projected[:, 0]], axis=0).astype(jnp.float32)
    query = short_filter[0, 0] * q[2:] + short_filter[1, 0] * q[1:-1] + short_filter[2, 0] * q[:-2]

    blocks = product.reshape(tok_rows // span + 1, span, groups, channels // groups)
    window = jnp.concatenate([blocks[:-1], blocks[1:]], axis=1)
    toeplitz = toeplitz_blocks(long_filter)
    filtered = jnp.einsum(
        "gij,bjgc->bigc", toeplitz, window, preferred_element_type=jnp.float32
    ).reshape(tok_rows, channels)
    gated = (query * filtered).astype(jnp.bfloat16)

    own = line_slots(gated, "zl", 4)
    other = lax.ppermute(own, "c", [(0, 1), (1, 0)])
    zl = lax.axis_index("zl")
    core = lax.axis_index("c")
    sources = (zl + jnp.arange(4, dtype=jnp.int32)) % 4

    def table_for(c):
        w = 2 * sources + c
        return jnp.stack([w % 4, (w // 4 + zh) % 2]).astype(jnp.int32)

    weight = weight_xy.reshape(4, 8, *weight_xy.shape[1:])
    table = jnp.concatenate([table_for(core), table_for(1 - core)], axis=1)
    return block_matmul(table, own, other, weight)


def solution(mesh):
    names = SEQ + WIDTH
    sizes = tuple(s for _, s in SEQ_PARTS + WIDTH_PARTS)
    fine = Mesh(mesh.devices.reshape(sizes), names)
    in_specs = (
        P(SEQ, None, WIDTH),
        P(None, None, WIDTH),
        P(WIDTH, None),
        P(SEQ, WIDTH),
    )
    out_specs = P(SEQ, WIDTH)
    return jax.shard_map(
        on_device, mesh=fine, in_specs=in_specs, out_specs=out_specs, check_vma=False
    )
```

```python
import jax
import jax.numpy as jnp
from jax import lax
from jax.experimental import pallas as pl
from jax.experimental.pallas import tpu as pltpu
from jax.sharding import Mesh
from jax.sharding import PartitionSpec as P

SEQ_PARTS = (("zh", 2), ("x", 4), ("y", 8))
WIDTH_PARTS = (("zl", 4), ("c", 2))
SEQ = tuple(n for n, _ in SEQ_PARTS)
WIDTH = tuple(n for n, _ in WIDTH_PARTS)


def from_behind(array):
    total = 1
    for _, size in SEQ_PARTS:
        total *= size
    pairs = [(i, i + 1) for i in range(total - 1)]
    return lax.ppermute(array, SEQ, pairs)


def toeplitz_kernel(row_ref, out_ref):
    groups, span, width = out_ref.shape
    period = row_ref.shape[1]

    def one_group(g, carry):
        row = row_ref[pl.ds(g, 1), :]
        tiled = jnp.broadcast_to(row, (span, period))
        rolled = pltpu.roll(tiled, shift=0, axis=1, stride=1, stride_axis=0)
        out_ref[g] = rolled[:, :width].astype(out_ref.dtype)
        return carry

    lax.fori_loop(0, groups, one_group, 0)


def toeplitz_blocks(long_filter):
    groups, span = long_filter.shape
    period = 3 * span
    row = jnp.concatenate(
        [
            jnp.zeros((groups, 1), jnp.float32),
            long_filter[:, ::-1].astype(jnp.float32),
            jnp.zeros((groups, period - span - 1), jnp.float32),
        ],
        axis=1,
    )
    return pl.pallas_call(
        toeplitz_kernel,
        out_shape=jax.ShapeDtypeStruct((groups, span, 2 * span), long_filter.dtype),
    )(row)


def line_slots(block, axis_name, size):
    index = lax.axis_index(axis_name)
    received = {}
    for offset in range(1, size):
        for d in (offset, -offset):
            pairs = [(i, i + d) for i in range(size) if 0 <= i + d < size]
            received[d] = lax.ppermute(block, axis_name, pairs)
    slots = [block]
    for k in range(1, size):
        slots.append(jnp.where(index + k < size, received[-k], received[size - k]))
    return jnp.stack(slots)


def matmul_kernel(table_ref, own_ref, other_ref, weight_a_ref, weight_b_ref, out_ref, acc_ref):
    k = pl.program_id(0)
    half = pl.num_programs(0) // 2

    @pl.when(k == 0)
    def _():
        acc_ref[...] = jnp.zeros_like(acc_ref)

    @pl.when(k < half)
    def _():
        acc_ref[...] += two_blocks(own_ref, 2 * k, weight_a_ref, weight_b_ref)

    @pl.when(k >= half)
    def _():
        acc_ref[...] += two_blocks(other_ref, 2 * (k - half), weight_a_ref, weight_b_ref)

    @pl.when(k == pl.num_programs(0) - 1)
    def _():
        out_ref[...] = acc_ref[...].astype(out_ref.dtype)


def two_blocks(piece_ref, first, weight_a_ref, weight_b_ref):
    rows_a = weight_a_ref[0, :, 0]
    rows_b = weight_b_ref[0, :, 0]
    rows_a = rows_a.reshape(-1, rows_a.shape[-1])
    rows_b = rows_b.reshape(-1, rows_b.shape[-1])
    total = jnp.dot(piece_ref[first], rows_a, preferred_element_type=jnp.float32)
    return total + jnp.dot(piece_ref[first + 1], rows_b, preferred_element_type=jnp.float32)


def block_matmul(table, own, other, weight):
    n, tok, width = own.shape
    _, ys, _, rows, cols = weight.shape
    steps = n // 2
    in_specs = [
        pl.BlockSpec(memory_space=pltpu.VMEM),
        pl.BlockSpec(memory_space=pltpu.VMEM),
        pl.BlockSpec((1, ys, 1, rows, cols), lambda k, t: (t[0, 2 * k], 0, t[1, 2 * k], 0, 0)),
        pl.BlockSpec((1, ys, 1, rows, cols), lambda k, t: (t[0, 2 * k + 1], 0, t[1, 2 * k + 1], 0, 0)),
    ]
    grid_spec = pltpu.PrefetchScalarGridSpec(
        num_scalar_prefetch=1,
        grid=(2 * steps,),
        in_specs=in_specs,
        out_specs=pl.BlockSpec((tok, cols), lambda k, t: (0, 0)),
        scratch_shapes=[pltpu.VMEM((tok, cols), jnp.float32)],
    )
    return pl.pallas_call(
        matmul_kernel,
        grid_spec=grid_spec,
        out_shape=jax.ShapeDtypeStruct((tok, cols), jnp.bfloat16),
    )(table, own, other, weight, weight)


def on_device(projected, short_filter, long_filter, out_weight):
    tok_rows = projected.shape[0]
    groups, span = long_filter.shape
    channels = projected.shape[2]

    partner = lax.ppermute(out_weight, "zh", [(0, 1), (1, 0)])
    zh = lax.axis_index("zh")
    pair = jnp.stack([out_weight, partner])
    weight_xy = lax.all_gather(pair, ("x", "y"), axis=0, tiled=False)

    kv_tail = projected[tok_rows - span - 2 :, 1:]
    q_tail = projected[tok_rows - 2 :, 0][None]
    received = from_behind(jnp.concatenate([kv_tail, q_tail], axis=0))
    kv = jnp.concatenate([received[: span + 2], projected[:, 1:]], axis=0).astype(jnp.float32)
    f_kv = short_filter[0, 1:] * kv[2:] + short_filter[1, 1:] * kv[1:-1] + short_filter[2, 1:] * kv[:-2]
    product = (f_kv[:, 0] * f_kv[:, 1]).astype(jnp.bfloat16)
    q = jnp.concatenate([received[span + 2], projected[:, 0]], axis=0).astype(jnp.float32)
    query = short_filter[0, 0] * q[2:] + short_filter[1, 0] * q[1:-1] + short_filter[2, 0] * q[:-2]

    blocks = product.reshape(tok_rows // span + 1, span, groups, channels // groups)
    window = jnp.concatenate([blocks[:-1], blocks[1:]], axis=1)
    toeplitz = toeplitz_blocks(long_filter)
    filtered = jnp.einsum(
        "gij,bjgc->bigc", toeplitz, window, preferred_element_type=jnp.float32
    ).reshape(tok_rows, channels)
    gated = (query * filtered).astype(jnp.bfloat16)

    own = line_slots(gated, "zl", 4)
    other = lax.ppermute(own, "c", [(0, 1), (1, 0)])
    zl = lax.axis_index("zl")
    core = lax.axis_index("c")
    sources = (zl + jnp.arange(4, dtype=jnp.int32)) % 4

    def table_for(c):
        w = 2 * sources + c
        return jnp.stack([w % 4, (w // 4 + zh) % 2]).astype(jnp.int32)

    weight = weight_xy.reshape(4, 8, *weight_xy.shape[1:])
    table = jnp.concatenate([table_for(core), table_for(1 - core)], axis=1)
    return block_matmul(table, own, other, weight)


def solution(mesh):
    names = SEQ + WIDTH
    sizes = tuple(s for _, s in SEQ_PARTS + WIDTH_PARTS)
    fine = Mesh(mesh.devices.reshape(sizes), names)
    in_specs = (
        P(SEQ, None, WIDTH),
        P(None, None, WIDTH),
        P(WIDTH, None),
        P(SEQ, WIDTH),
    )
    out_specs = P(SEQ, WIDTH)
    return jax.shard_map(
        on_device, mesh=fine, in_specs=in_specs, out_specs=out_specs, check_vma=False
    )
```

```python
import jax
import jax.numpy as jnp
from jax import lax
from jax.experimental import pallas as pl
from jax.experimental.pallas import tpu as pltpu
from jax.sharding import Mesh
from jax.sharding import PartitionSpec as P

SEQ_PARTS = (("zh", 2), ("x", 4), ("y", 8))
WIDTH_PARTS = (("zl", 4), ("c", 2))
SEQ = tuple(n for n, _ in SEQ_PARTS)
WIDTH = tuple(n for n, _ in WIDTH_PARTS)


def from_behind(array):
    total = 1
    for _, size in SEQ_PARTS:
        total *= size
    pairs = [(i, i + 1) for i in range(total - 1)]
    return lax.ppermute(array, SEQ, pairs)


def toeplitz_kernel(row_ref, out_ref):
    groups, span, width = out_ref.shape
    period = row_ref.shape[1]

    def one_group(g, carry):
        row = row_ref[pl.ds(g, 1), :]
        tiled = jnp.broadcast_to(row, (span, period))
        rolled = pltpu.roll(tiled, shift=0, axis=1, stride=1, stride_axis=0)
        out_ref[g] = rolled[:, :width].astype(out_ref.dtype)
        return carry

    lax.fori_loop(0, groups, one_group, 0)


def toeplitz_blocks(long_filter):
    groups, span = long_filter.shape
    period = 3 * span
    row = jnp.concatenate(
        [
            jnp.zeros((groups, 1), jnp.float32),
            long_filter[:, ::-1].astype(jnp.float32),
            jnp.zeros((groups, period - span - 1), jnp.float32),
        ],
        axis=1,
    )
    return pl.pallas_call(
        toeplitz_kernel,
        out_shape=jax.ShapeDtypeStruct((groups, span, 2 * span), long_filter.dtype),
    )(row)


def line_slots(block, axis_name, size):
    slots = [block]
    for k in range(1, size):
        shift = size - k
        pairs = [(i, (i + shift) % size) for i in range(size)]
        slots.append(lax.ppermute(block, axis_name, pairs))
    return jnp.stack(slots)


def matmul_kernel(table_ref, own_ref, other_ref, weight_a_ref, weight_b_ref, out_ref, acc_ref):
    k = pl.program_id(0)
    half = pl.num_programs(0) // 2

    @pl.when(k == 0)
    def _():
        acc_ref[...] = jnp.zeros_like(acc_ref)

    @pl.when(k < half)
    def _():
        acc_ref[...] += two_blocks(own_ref, weight_a_ref, weight_b_ref)

    @pl.when(k >= half)
    def _():
        acc_ref[...] += two_blocks(other_ref, weight_a_ref, weight_b_ref)

    @pl.when(k == pl.num_programs(0) - 1)
    def _():
        out_ref[...] = acc_ref[...].astype(out_ref.dtype)


def two_blocks(piece_ref, weight_a_ref, weight_b_ref):
    rows_a = weight_a_ref[0, :, 0]
    rows_b = weight_b_ref[0, :, 0]
    rows_a = rows_a.reshape(-1, rows_a.shape[-1])
    rows_b = rows_b.reshape(-1, rows_b.shape[-1])
    total = jnp.dot(piece_ref[0], rows_a, preferred_element_type=jnp.float32)
    return total + jnp.dot(piece_ref[1], rows_b, preferred_element_type=jnp.float32)


def block_matmul(table, own, other, weight):
    n, tok, width = own.shape
    _, ys, _, rows, cols = weight.shape
    steps = n // 2
    in_specs = [
        pl.BlockSpec((2, tok, width), lambda k, t: (jnp.minimum(k, steps - 1), 0, 0)),
        pl.BlockSpec((2, tok, width), lambda k, t: (jnp.maximum(k - steps, 0), 0, 0)),
        pl.BlockSpec((1, ys, 1, rows, cols), lambda k, t: (t[0, 2 * k], 0, t[1, 2 * k], 0, 0)),
        pl.BlockSpec((1, ys, 1, rows, cols), lambda k, t: (t[0, 2 * k + 1], 0, t[1, 2 * k + 1], 0, 0)),
    ]
    grid_spec = pltpu.PrefetchScalarGridSpec(
        num_scalar_prefetch=1,
        grid=(2 * steps,),
        in_specs=in_specs,
        out_specs=pl.BlockSpec((tok, cols), lambda k, t: (0, 0)),
        scratch_shapes=[pltpu.VMEM((tok, cols), jnp.float32)],
    )
    return pl.pallas_call(
        matmul_kernel,
        grid_spec=grid_spec,
        out_shape=jax.ShapeDtypeStruct((tok, cols), jnp.bfloat16),
    )(table, own, other, weight, weight)


def on_device(projected, short_filter, long_filter, out_weight):
    tok_rows = projected.shape[0]
    groups, span = long_filter.shape
    channels = projected.shape[2]

    partner = lax.ppermute(out_weight, "zh", [(0, 1), (1, 0)])
    zh = lax.axis_index("zh")
    pair = jnp.stack([out_weight, partner])
    weight_xy = lax.all_gather(pair, ("x", "y"), axis=0, tiled=False)

    kv_tail = projected[tok_rows - span - 2 :, 1:]
    q_tail = projected[tok_rows - 2 :, 0][None]
    received = from_behind(jnp.concatenate([kv_tail, q_tail], axis=0))
    kv = jnp.concatenate([received[: span + 2], projected[:, 1:]], axis=0).astype(jnp.float32)
    f_kv = short_filter[0, 1:] * kv[2:] + short_filter[1, 1:] * kv[1:-1] + short_filter[2, 1:] * kv[:-2]
    product = (f_kv[:, 0] * f_kv[:, 1]).astype(jnp.bfloat16)
    q = jnp.concatenate([received[span + 2], projected[:, 0]], axis=0).astype(jnp.float32)
    query = short_filter[0, 0] * q[2:] + short_filter[1, 0] * q[1:-1] + short_filter[2, 0] * q[:-2]

    blocks = product.reshape(tok_rows // span + 1, span, groups, channels // groups)
    window = jnp.concatenate([blocks[:-1], blocks[1:]], axis=1)
    toeplitz = toeplitz_blocks(long_filter)
    filtered = jnp.einsum(
        "gij,bjgc->bigc", toeplitz, window, preferred_element_type=jnp.float32
    ).reshape(tok_rows, channels)
    gated = (query * filtered).astype(jnp.bfloat16)

    own = line_slots(gated, "zl", 4)
    other = lax.ppermute(own, "c", [(0, 1), (1, 0)])
    zl = lax.axis_index("zl")
    core = lax.axis_index("c")
    sources = (zl + jnp.arange(4, dtype=jnp.int32)) % 4

    def table_for(c):
        w = 2 * sources + c
        return jnp.stack([w % 4, (w // 4 + zh) % 2]).astype(jnp.int32)

    weight = weight_xy.reshape(4, 8, *weight_xy.shape[1:])
    table = jnp.concatenate([table_for(core), table_for(1 - core)], axis=1)
    return block_matmul(table, own, other, weight)


def solution(mesh):
    names = SEQ + WIDTH
    sizes = tuple(s for _, s in SEQ_PARTS + WIDTH_PARTS)
    fine = Mesh(mesh.devices.reshape(sizes), names)
    in_specs = (
        P(SEQ, None, WIDTH),
        P(None, None, WIDTH),
        P(WIDTH, None),
        P(SEQ, WIDTH),
    )
    out_specs = P(SEQ, WIDTH)
    return jax.shard_map(
        on_device, mesh=fine, in_specs=in_specs, out_specs=out_specs, check_vma=False
    )
```

```python
import jax
import jax.numpy as jnp
from jax import lax
from jax.experimental import pallas as pl
from jax.experimental.pallas import tpu as pltpu
from jax.sharding import Mesh
from jax.sharding import PartitionSpec as P

SEQ_PARTS = (("zh", 2), ("x", 4), ("y", 8))
WIDTH_PARTS = (("zl", 4), ("c", 2))
SEQ = tuple(n for n, _ in SEQ_PARTS)
WIDTH = tuple(n for n, _ in WIDTH_PARTS)


def from_behind(array):
    total = 1
    for _, size in SEQ_PARTS:
        total *= size
    pairs = [(i, i + 1) for i in range(total - 1)]
    return lax.ppermute(array, SEQ, pairs)


def toeplitz_kernel(row_ref, out_ref):
    groups, span, width = out_ref.shape
    period = row_ref.shape[1]

    def one_group(g, carry):
        row = row_ref[pl.ds(g, 1), :]
        tiled = jnp.broadcast_to(row, (span, period))
        rolled = pltpu.roll(tiled, shift=0, axis=1, stride=1, stride_axis=0)
        out_ref[g] = rolled[:, :width].astype(out_ref.dtype)
        return carry

    lax.fori_loop(0, groups, one_group, 0)


def toeplitz_blocks(long_filter):
    groups, span = long_filter.shape
    period = 3 * span
    row = jnp.concatenate(
        [
            jnp.zeros((groups, 1), jnp.float32),
            long_filter[:, ::-1].astype(jnp.float32),
            jnp.zeros((groups, period - span - 1), jnp.float32),
        ],
        axis=1,
    )
    return pl.pallas_call(
        toeplitz_kernel,
        out_shape=jax.ShapeDtypeStruct((groups, span, 2 * span), long_filter.dtype),
    )(row)


def line_slots(block, axis_name, size):
    slots = [block]
    for k in range(1, size):
        shift = size - k
        pairs = [(i, (i + shift) % size) for i in range(size)]
        slots.append(lax.ppermute(block, axis_name, pairs))
    return jnp.stack(slots)


def matmul_kernel(table_ref, own_ref, other_ref, weight_a_ref, weight_b_ref, out_ref, acc_ref):
    k = pl.program_id(0)
    half = pl.num_programs(0) // 2

    @pl.when(k == 0)
    def _():
        acc_ref[...] = jnp.zeros_like(acc_ref)

    @pl.when(k < half)
    def _():
        acc_ref[...] += two_blocks(own_ref, weight_a_ref, weight_b_ref)

    @pl.when(k >= half)
    def _():
        acc_ref[...] += two_blocks(other_ref, weight_a_ref, weight_b_ref)

    @pl.when(k == pl.num_programs(0) - 1)
    def _():
        out_ref[...] = acc_ref[...].astype(out_ref.dtype)


def two_blocks(piece_ref, weight_a_ref, weight_b_ref):
    rows_a = weight_a_ref[0, :, 0]
    rows_b = weight_b_ref[0, :, 0]
    rows_a = rows_a.reshape(-1, rows_a.shape[-1])
    rows_b = rows_b.reshape(-1, rows_b.shape[-1])
    total = jnp.dot(piece_ref[0], rows_a, preferred_element_type=jnp.float32)
    return total + jnp.dot(piece_ref[1], rows_b, preferred_element_type=jnp.float32)


def block_matmul(table, own, other, weight):
    n, tok, width = own.shape
    _, ys, _, rows, cols = weight.shape
    steps = n // 2
    in_specs = [
        pl.BlockSpec((2, tok, width), lambda k, t: (jnp.minimum(k, steps - 1), 0, 0)),
        pl.BlockSpec((2, tok, width), lambda k, t: (jnp.maximum(k - steps, 0), 0, 0)),
        pl.BlockSpec((1, ys, 1, rows, cols), lambda k, t: (t[0, 2 * k], 0, t[1, 2 * k], 0, 0)),
        pl.BlockSpec((1, ys, 1, rows, cols), lambda k, t: (t[0, 2 * k + 1], 0, t[1, 2 * k + 1], 0, 0)),
    ]
    grid_spec = pltpu.PrefetchScalarGridSpec(
        num_scalar_prefetch=1,
        grid=(2 * steps,),
        in_specs=in_specs,
        out_specs=pl.BlockSpec((tok, cols), lambda k, t: (0, 0)),
        scratch_shapes=[pltpu.VMEM((tok, cols), jnp.float32)],
    )
    return pl.pallas_call(
        matmul_kernel,
        grid_spec=grid_spec,
        out_shape=jax.ShapeDtypeStruct((tok, cols), jnp.bfloat16),
    )(table, own, other, weight, weight)


def on_device(projected, short_filter, long_filter, out_weight):
    tok_rows = projected.shape[0]
    groups, span = long_filter.shape
    channels = projected.shape[2]

    pair = jnp.stack([out_weight, jnp.zeros_like(out_weight)])
    pair, sent = lax.optimization_barrier((pair, out_weight))
    partner = lax.ppermute(sent, "zh", [(0, 1), (1, 0)])
    zh = lax.axis_index("zh")
    pair = lax.dynamic_update_index_in_dim(pair, partner, 1, 0)
    weight_xy = lax.all_gather(pair, ("x", "y"), axis=0, tiled=False)

    kv_tail = projected[tok_rows - span - 2 :, 1:]
    q_tail = projected[tok_rows - 2 :, 0][None]
    received = from_behind(jnp.concatenate([kv_tail, q_tail], axis=0))
    kv = jnp.concatenate([received[: span + 2], projected[:, 1:]], axis=0).astype(jnp.float32)
    f_kv = short_filter[0, 1:] * kv[2:] + short_filter[1, 1:] * kv[1:-1] + short_filter[2, 1:] * kv[:-2]
    product = (f_kv[:, 0] * f_kv[:, 1]).astype(jnp.bfloat16)
    q = jnp.concatenate([received[span + 2], projected[:, 0]], axis=0).astype(jnp.float32)
    query = short_filter[0, 0] * q[2:] + short_filter[1, 0] * q[1:-1] + short_filter[2, 0] * q[:-2]

    blocks = product.reshape(tok_rows // span + 1, span, groups, channels // groups)
    window = jnp.concatenate([blocks[:-1], blocks[1:]], axis=1)
    toeplitz = toeplitz_blocks(long_filter)
    filtered = jnp.einsum(
        "gij,bjgc->bigc", toeplitz, window, preferred_element_type=jnp.float32
    ).reshape(tok_rows, channels)
    gated = (query * filtered).astype(jnp.bfloat16)

    own = line_slots(gated, "zl", 4)
    other = lax.ppermute(own, "c", [(0, 1), (1, 0)])
    zl = lax.axis_index("zl")
    core = lax.axis_index("c")
    sources = (zl + jnp.arange(4, dtype=jnp.int32)) % 4

    def table_for(c):
        w = 2 * sources + c
        return jnp.stack([w % 4, (w // 4 + zh) % 2]).astype(jnp.int32)

    weight = weight_xy.reshape(4, 8, *weight_xy.shape[1:])
    table = jnp.concatenate([table_for(core), table_for(1 - core)], axis=1)
    return block_matmul(table, own, other, weight)


def solution(mesh):
    names = SEQ + WIDTH
    sizes = tuple(s for _, s in SEQ_PARTS + WIDTH_PARTS)
    fine = Mesh(mesh.devices.reshape(sizes), names)
    in_specs = (
        P(SEQ, None, WIDTH),
        P(None, None, WIDTH),
        P(WIDTH, None),
        P(SEQ, WIDTH),
    )
    out_specs = P(SEQ, WIDTH)
    return jax.shard_map(
        on_device, mesh=fine, in_specs=in_specs, out_specs=out_specs, check_vma=False
    )
```

```python
import jax
import jax.numpy as jnp
from jax import lax
from jax.experimental import pallas as pl
from jax.experimental.pallas import tpu as pltpu
from jax.sharding import Mesh
from jax.sharding import PartitionSpec as P

SEQ_PARTS = (("zh", 2), ("x", 4), ("y", 8))
WIDTH_PARTS = (("zl", 4), ("c", 2))
SEQ = tuple(n for n, _ in SEQ_PARTS)
WIDTH = tuple(n for n, _ in WIDTH_PARTS)


def from_behind(array):
    total = 1
    for _, size in SEQ_PARTS:
        total *= size
    pairs = [(i, i + 1) for i in range(total - 1)]
    return lax.ppermute(array, SEQ, pairs)


def toeplitz_kernel(row_ref, out_ref):
    groups, span, width = out_ref.shape
    period = row_ref.shape[1]

    def one_group(g, carry):
        row = row_ref[pl.ds(g, 1), :]
        tiled = jnp.broadcast_to(row, (span, period))
        rolled = pltpu.roll(tiled, shift=0, axis=1, stride=1, stride_axis=0)
        out_ref[g] = rolled[:, :width].astype(out_ref.dtype)
        return carry

    lax.fori_loop(0, groups, one_group, 0)


def toeplitz_blocks(long_filter):
    groups, span = long_filter.shape
    period = 3 * span
    row = jnp.concatenate(
        [
            jnp.zeros((groups, 1), jnp.float32),
            long_filter[:, ::-1].astype(jnp.float32),
            jnp.zeros((groups, period - span - 1), jnp.float32),
        ],
        axis=1,
    )
    return pl.pallas_call(
        toeplitz_kernel,
        out_shape=jax.ShapeDtypeStruct((groups, span, 2 * span), long_filter.dtype),
    )(row)


def line_slots(block, axis_name, size):
    slots = [block]
    for k in range(1, size):
        shift = size - k
        pairs = [(i, (i + shift) % size) for i in range(size)]
        slots.append(lax.ppermute(block, axis_name, pairs))
    return jnp.stack(slots)


def matmul_kernel(table_ref, own_ref, other_ref, weight_a_ref, weight_b_ref, out_ref, acc_ref):
    k = pl.program_id(0)
    half = pl.num_programs(0) // 2
    flip = table_ref[2, 0]

    @pl.when(k == 0)
    def _():
        acc_ref[...] = jnp.zeros_like(acc_ref)

    for pieces, first in ((own_ref, True), (other_ref, False)):
        for turned in (False, True):

            @pl.when(((k < half) == first) & ((flip == 1) == turned))
            def _(pieces=pieces, turned=turned):
                acc_ref[...] += two_blocks(pieces, weight_a_ref, weight_b_ref, turned)

    @pl.when(k == pl.num_programs(0) - 1)
    def _():
        out_ref[...] = acc_ref[...].astype(out_ref.dtype)


def rows_of(weight_ref, turned):
    ys = weight_ref.shape[1]
    order = range(ys - 1, -1, -1) if turned else range(ys)
    return jnp.concatenate([weight_ref[0, y, 0] for y in order], axis=0)


def two_blocks(piece_ref, weight_a_ref, weight_b_ref, turned):
    total = jnp.dot(piece_ref[0], rows_of(weight_a_ref, turned), preferred_element_type=jnp.float32)
    return total + jnp.dot(piece_ref[1], rows_of(weight_b_ref, turned), preferred_element_type=jnp.float32)


def block_matmul(table, own, other, weight):
    n, tok, width = own.shape
    _, ys, _, rows, cols = weight.shape
    steps = n // 2
    in_specs = [
        pl.BlockSpec((2, tok, width), lambda k, t: (jnp.minimum(k, steps - 1), 0, 0)),
        pl.BlockSpec((2, tok, width), lambda k, t: (jnp.maximum(k - steps, 0), 0, 0)),
        pl.BlockSpec((1, ys, 1, rows, cols), lambda k, t: (t[0, 2 * k], 0, t[1, 2 * k], 0, 0)),
        pl.BlockSpec((1, ys, 1, rows, cols), lambda k, t: (t[0, 2 * k + 1], 0, t[1, 2 * k + 1], 0, 0)),
    ]
    grid_spec = pltpu.PrefetchScalarGridSpec(
        num_scalar_prefetch=1,
        grid=(2 * steps,),
        in_specs=in_specs,
        out_specs=pl.BlockSpec((tok, cols), lambda k, t: (0, 0)),
        scratch_shapes=[pltpu.VMEM((tok, cols), jnp.float32)],
    )
    return pl.pallas_call(
        matmul_kernel,
        grid_spec=grid_spec,
        out_shape=jax.ShapeDtypeStruct((tok, cols), jnp.bfloat16),
    )(table, own, other, weight, weight)


def on_device(projected, short_filter, long_filter, out_weight):
    tok_rows = projected.shape[0]
    groups, span = long_filter.shape
    channels = projected.shape[2]

    pair = jnp.stack([out_weight, jnp.zeros_like(out_weight)])
    pair, sent = lax.optimization_barrier((pair, out_weight))
    partner = lax.ppermute(sent, "zh", [(0, 1), (1, 0)])
    zh = lax.axis_index("zh")
    pair = lax.dynamic_update_index_in_dim(pair, partner, 1, 0)
    order = [(x * 8 + y) * 2 for x in range(4) for y in range(8)]
    turned = [(x * 8 + (7 - y)) * 2 + 1 for x in range(4) for y in range(8)]
    weight_xy = lax.all_gather(
        pair, ("x", "y", "c"), axis=0, tiled=False, axis_index_groups=[order, turned]
    )

    kv_tail = projected[tok_rows - span - 2 :, 1:]
    q_tail = projected[tok_rows - 2 :, 0][None]
    received = from_behind(jnp.concatenate([kv_tail, q_tail], axis=0))
    kv = jnp.concatenate([received[: span + 2], projected[:, 1:]], axis=0).astype(jnp.float32)
    f_kv = short_filter[0, 1:] * kv[2:] + short_filter[1, 1:] * kv[1:-1] + short_filter[2, 1:] * kv[:-2]
    product = (f_kv[:, 0] * f_kv[:, 1]).astype(jnp.bfloat16)
    q = jnp.concatenate([received[span + 2], projected[:, 0]], axis=0).astype(jnp.float32)
    query = short_filter[0, 0] * q[2:] + short_filter[1, 0] * q[1:-1] + short_filter[2, 0] * q[:-2]

    blocks = product.reshape(tok_rows // span + 1, span, groups, channels // groups)
    window = jnp.concatenate([blocks[:-1], blocks[1:]], axis=1)
    toeplitz = toeplitz_blocks(long_filter)
    filtered = jnp.einsum(
        "gij,bjgc->bigc", toeplitz, window, preferred_element_type=jnp.float32
    ).reshape(tok_rows, channels)
    gated = (query * filtered).astype(jnp.bfloat16)

    own = line_slots(gated, "zl", 4)
    other = lax.ppermute(own, "c", [(0, 1), (1, 0)])
    zl = lax.axis_index("zl")
    core = lax.axis_index("c")
    sources = (zl + jnp.arange(4, dtype=jnp.int32)) % 4

    def table_for(c):
        w = 2 * sources + c
        return jnp.stack([w % 4, (w // 4 + zh) % 2]).astype(jnp.int32)

    weight = weight_xy.reshape(4, 8, *weight_xy.shape[1:])
    table = jnp.concatenate([table_for(core), table_for(1 - core)], axis=1)
    table = jnp.concatenate([table, jnp.broadcast_to(core, (1, table.shape[1])).astype(jnp.int32)])
    return block_matmul(table, own, other, weight)


def solution(mesh):
    names = SEQ + WIDTH
    sizes = tuple(s for _, s in SEQ_PARTS + WIDTH_PARTS)
    fine = Mesh(mesh.devices.reshape(sizes), names)
    in_specs = (
        P(SEQ, None, WIDTH),
        P(None, None, WIDTH),
        P(WIDTH, None),
        P(SEQ, WIDTH),
    )
    out_specs = P(SEQ, WIDTH)
    return jax.shard_map(
        on_device, mesh=fine, in_specs=in_specs, out_specs=out_specs, check_vma=False
    )
```

```python
import jax
import jax.numpy as jnp
from jax import lax
from jax.experimental import pallas as pl
from jax.experimental.pallas import tpu as pltpu
from jax.sharding import Mesh
from jax.sharding import PartitionSpec as P

SEQ_PARTS = (("zh", 2), ("x", 4), ("y", 8))
WIDTH_PARTS = (("zl", 4), ("c", 2))
SEQ = tuple(n for n, _ in SEQ_PARTS)
WIDTH = tuple(n for n, _ in WIDTH_PARTS)


def from_behind(array):
    total = 1
    for _, size in SEQ_PARTS:
        total *= size
    pairs = [(i, i + 1) for i in range(total - 1)]
    return lax.ppermute(array, SEQ, pairs)


def toeplitz_kernel(row_ref, out_ref):
    groups, span, width = out_ref.shape
    period = row_ref.shape[1]

    def one_group(g, carry):
        row = row_ref[pl.ds(g, 1), :]
        tiled = jnp.broadcast_to(row, (span, period))
        rolled = pltpu.roll(tiled, shift=0, axis=1, stride=1, stride_axis=0)
        out_ref[g] = rolled[:, :width].astype(out_ref.dtype)
        return carry

    lax.fori_loop(0, groups, one_group, 0)


def toeplitz_blocks(long_filter):
    groups, span = long_filter.shape
    period = 3 * span
    row = jnp.concatenate(
        [
            jnp.zeros((groups, 1), jnp.float32),
            long_filter[:, ::-1].astype(jnp.float32),
            jnp.zeros((groups, period - span - 1), jnp.float32),
        ],
        axis=1,
    )
    return pl.pallas_call(
        toeplitz_kernel,
        out_shape=jax.ShapeDtypeStruct((groups, span, 2 * span), long_filter.dtype),
    )(row)


def line_slots(block, axis_name, size):
    slots = [block]
    for k in range(1, size):
        shift = size - k
        pairs = [(i, (i + shift) % size) for i in range(size)]
        slots.append(lax.ppermute(block, axis_name, pairs))
    return jnp.stack(slots)


def matmul_kernel(table_ref, own_ref, other_ref, weight_a_ref, weight_b_ref, out_ref, acc_ref):
    k = pl.program_id(0)
    half = pl.num_programs(0) // 2

    @pl.when(k == 0)
    def _():
        acc_ref[...] = jnp.zeros_like(acc_ref)

    @pl.when(k < half)
    def _():
        acc_ref[...] += two_blocks(own_ref, weight_a_ref, weight_b_ref)

    @pl.when(k >= half)
    def _():
        acc_ref[...] += two_blocks(other_ref, weight_a_ref, weight_b_ref)

    @pl.when(k == pl.num_programs(0) - 1)
    def _():
        out_ref[...] = acc_ref[...].astype(out_ref.dtype)


def two_blocks(piece_ref, weight_a_ref, weight_b_ref):
    rows_a = weight_a_ref[:, 0, 0]
    rows_b = weight_b_ref[:, 0, 0]
    rows_a = rows_a.reshape(-1, rows_a.shape[-1])
    rows_b = rows_b.reshape(-1, rows_b.shape[-1])
    total = jnp.dot(piece_ref[0], rows_a, preferred_element_type=jnp.float32)
    return total + jnp.dot(piece_ref[1], rows_b, preferred_element_type=jnp.float32)


def block_matmul(table, own, other, weight):
    n, tok, width = own.shape
    ys, _, _, rows, cols = weight.shape
    steps = n // 2
    in_specs = [
        pl.BlockSpec((2, tok, width), lambda k, t: (jnp.minimum(k, steps - 1), 0, 0)),
        pl.BlockSpec((2, tok, width), lambda k, t: (jnp.maximum(k - steps, 0), 0, 0)),
        pl.BlockSpec((ys, 1, 1, rows, cols), lambda k, t: (0, t[0, 2 * k], t[1, 2 * k], 0, 0)),
        pl.BlockSpec((ys, 1, 1, rows, cols), lambda k, t: (0, t[0, 2 * k + 1], t[1, 2 * k + 1], 0, 0)),
    ]
    grid_spec = pltpu.PrefetchScalarGridSpec(
        num_scalar_prefetch=1,
        grid=(2 * steps,),
        in_specs=in_specs,
        out_specs=pl.BlockSpec((tok, cols), lambda k, t: (0, 0)),
        scratch_shapes=[pltpu.VMEM((tok, cols), jnp.float32)],
    )
    return pl.pallas_call(
        matmul_kernel,
        grid_spec=grid_spec,
        out_shape=jax.ShapeDtypeStruct((tok, cols), jnp.bfloat16),
    )(table, own, other, weight, weight)


def on_device(projected, short_filter, long_filter, out_weight):
    tok_rows = projected.shape[0]
    groups, span = long_filter.shape
    channels = projected.shape[2]

    pair = jnp.stack([out_weight, jnp.zeros_like(out_weight)])
    pair, sent = lax.optimization_barrier((pair, out_weight))
    partner = lax.ppermute(sent, "zh", [(0, 1), (1, 0)])
    zh = lax.axis_index("zh")
    pair = lax.dynamic_update_index_in_dim(pair, partner, 1, 0)
    weight_yx = lax.all_gather(pair, ("y", "x"), axis=0, tiled=False)

    kv_tail = projected[tok_rows - span - 2 :, 1:]
    q_tail = projected[tok_rows - 2 :, 0][None]
    received = from_behind(jnp.concatenate([kv_tail, q_tail], axis=0))
    kv = jnp.concatenate([received[: span + 2], projected[:, 1:]], axis=0).astype(jnp.float32)
    f_kv = short_filter[0, 1:] * kv[2:] + short_filter[1, 1:] * kv[1:-1] + short_filter[2, 1:] * kv[:-2]
    product = (f_kv[:, 0] * f_kv[:, 1]).astype(jnp.bfloat16)
    q = jnp.concatenate([received[span + 2], projected[:, 0]], axis=0).astype(jnp.float32)
    query = short_filter[0, 0] * q[2:] + short_filter[1, 0] * q[1:-1] + short_filter[2, 0] * q[:-2]

    blocks = product.reshape(tok_rows // span + 1, span, groups, channels // groups)
    window = jnp.concatenate([blocks[:-1], blocks[1:]], axis=1)
    toeplitz = toeplitz_blocks(long_filter)
    filtered = jnp.einsum(
        "gij,bjgc->bigc", toeplitz, window, preferred_element_type=jnp.float32
    ).reshape(tok_rows, channels)
    gated = (query * filtered).astype(jnp.bfloat16)

    own = line_slots(gated, "zl", 4)
    other = lax.ppermute(own, "c", [(0, 1), (1, 0)])
    zl = lax.axis_index("zl")
    core = lax.axis_index("c")
    sources = (zl + jnp.arange(4, dtype=jnp.int32)) % 4

    def table_for(c):
        w = 2 * sources + c
        return jnp.stack([w % 4, (w // 4 + zh) % 2]).astype(jnp.int32)

    weight = weight_yx.reshape(8, 4, *weight_yx.shape[1:])
    table = jnp.concatenate([table_for(core), table_for(1 - core)], axis=1)
    return block_matmul(table, own, other, weight)


def solution(mesh):
    names = SEQ + WIDTH
    sizes = tuple(s for _, s in SEQ_PARTS + WIDTH_PARTS)
    fine = Mesh(mesh.devices.reshape(sizes), names)
    in_specs = (
        P(SEQ, None, WIDTH),
        P(None, None, WIDTH),
        P(WIDTH, None),
        P(SEQ, WIDTH),
    )
    out_specs = P(SEQ, WIDTH)
    return jax.shard_map(
        on_device, mesh=fine, in_specs=in_specs, out_specs=out_specs, check_vma=False
    )
```
